256 devices in a mesh: dp: 16 (over y_lo, z), tm: 16 (over y_hi, x, core).
Axes of the slice: x: 4, y: 4 (y_hi: 2, y_lo: 2; y = y_hi * 2 + y_lo), z: 8, core: 2. Of those that a mesh axis runs over, the one named last changes fastest.
Arguments:
- signal: bfloat16 [16, 32768, 256], P('dp', 'tm'), may hold values from -6 to 6
- timesteps: int32 [16], P('dp'), may hold values from 0 to 999
- cotangent: bfloat16 [16, 8192, 512], P('dp', 'tm'), may hold values from -6 to 6
- conv_one: bfloat16 [768, 256], replicated, may hold values from -0.21875 to 0.21875
- down_proj: bfloat16 [1024, 512], replicated, may hold values from -0.1875 to 0.1875
- conv_two: bfloat16 [1536, 512], replicated, may hold values from -0.15625 to 0.15625
- time_proj: bfloat16 [256, 256], replicated, may hold values from -0.375 to 0.375
Outputs:
- encoded: bfloat16 [16, 8192, 512], P('dp', 'tm')
- signal_grad: bfloat16 [16, 32768, 256], P('dp', 'tm')
- conv_one_grad: float32 [768, 256], P('dp', 'tm')
- down_proj_grad: float32 [1024, 512], P('dp', 'tm')
- conv_two_grad: float32 [1536, 512], P('dp', 'tm')
- time_proj_grad: float32 [256, 256], P('dp', 'tm')
The draws below stay inside these ranges and needn't reach their ends.
All inputs are finite; a program needn't handle non-finite values.
Results may differ from the reference program's by a relative error of at most 0.022.
Values may be sent and summed in bfloat16 or wider, within the bound.
No kernel may reach another device: no remote copies, remote signals or barrier semaphores. Data moves between devices by JAX's collectives and lax.ppermute only.
A program may use at most 64 MiB of HBM per device.

```python
import math
import jax
import jax.numpy as jnp
from jax import lax

CA = 256
CB = 512
EMB = 256
CLIPS = 16
LA = 32768
LB = 8192


def touch_ends(result, stream_key, least, largest):
    shape = result.shape
    place = [jax.random.randint(jax.random.fold_in(stream_key, axis), (), 0, shape[axis]) for axis in range(len(shape))]
    result = result.at[tuple(place)].set(least)
    longest = shape.index(max(shape))
    place[longest] = (place[longest] + 1) % shape[longest]
    return result.at[tuple(place)].set(largest)


def shard_levels(own_key, shape, shards, smallest, high):
    def one(position, shards_of):
        steps = jax.random.uniform(jax.random.fold_in(jax.random.fold_in(own_key, 6), position), (shards_of,), jnp.float32, smallest / len(shards), high / len(shards))
        return jnp.repeat(jnp.exp(steps), shape[position] // shards_of).reshape((-1,) + (1,) * (len(shape) - position - 1))

    factor_of = one(*shards[0])
    for cut in shards[1:]:
        factor_of = factor_of * one(*cut)
    return factor_of


def gaussian(key, shape, scale, limit, split=(), kind=jnp.bfloat16):
    result = jax.random.normal(key, shape, jnp.float32) * scale
    if len(split) > 0:
        result = shard_levels(key, shape, split, -0.22, 0.18) * result
    return jnp.clip(result, min=-limit, max=limit).astype(kind)


def setup_inputs(seed: int = 0) -> dict:
    seeds = jax.random.split(jax.random.key(seed), 8)
    signal = gaussian(seeds[0], (CLIPS, LA, CA), 1.0, 6.0, ((0, 16), (1, 16)))
    timesteps = touch_ends(jax.random.randint(seeds[1], (CLIPS,), 0, 1000), jax.random.fold_in(seeds[1], 1), 0, 999).astype(jnp.int32)
    cotangent = gaussian(seeds[2], (CLIPS, LB, CB), 1.0, 6.0, ((0, 16), (1, 16)))
    conv_one = gaussian(seeds[3], (3 * CA, CA), (3 * CA) ** -0.5, 0.21875)
    down_proj = gaussian(seeds[4], (4 * CA, CB), (4 * CA) ** -0.5, 0.1875)
    conv_two = gaussian(seeds[5], (3 * CB, CB), (3 * CB) ** -0.5, 0.15625)
    time_proj = gaussian(seeds[6], (EMB, CA), EMB ** -0.5, 0.375)
    return dict(signal=signal, timesteps=timesteps, cotangent=cotangent, conv_one=conv_one, down_proj=down_proj, conv_two=conv_two, time_proj=time_proj)


EPS = 1e-06

def rms_fwd(values):
    meansq = lax.optimization_barrier(jnp.mean(values * values, -1, keepdims=True))
    factor = lax.rsqrt(meansq + EPS)
    return (values * factor, factor)

def rms_back(dnorm, normed, factor):
    return factor * (dnorm - normed * lax.optimization_barrier(jnp.mean(dnorm * normed, -1, keepdims=True)))

def silu_slope(values):
    sigm = jax.nn.sigmoid(values)
    return sigm * (1.0 + values * (1.0 - sigm))

def embed(stamps, width):
    half = width // 2
    freqs = jnp.exp(-math.log(10000.0) * jnp.arange(half, dtype=jnp.float32) / half)
    angles = stamps.astype(jnp.float32)[:, None] * freqs[None, :]
    return jnp.concatenate([jnp.sin(angles), jnp.cos(angles)], axis=-1)

def unfold(padded, length):
    return jnp.concatenate([padded[offset:offset + length] for offset in range(3)], axis=-1)

def conv_back(padded, weight, length):
    width = weight.shape[0] // 3
    total = jnp.zeros((length, width), jnp.float32)
    for offset in range(3):
        total = total + lax.dot_general(padded[2 - offset:2 - offset + length], weight[offset * width:(offset + 1) * width], (((1,), (1,)), ((), ())), preferred_element_type=jnp.float32)
    return total

def reference(signal, timesteps, cotangent, conv_one, down_proj, conv_two, time_proj):
    emb_all = embed(timesteps, EMB)
    temb_all = jnp.dot(emb_all, time_proj.astype(jnp.float32), precision=lax.Precision.HIGHEST)

    def per_clip(carry, inputs):
        clip, emb_row, temb, grad_out = inputs
        x32 = clip.astype(jnp.float32)
        normed, factor = rms_fwd(x32)
        pre = normed + temb[None, :]
        act_a = jax.nn.silu(pre).astype(jnp.bfloat16)
        rows_a = unfold(jnp.pad(act_a, ((1, 1), (0, 0))), LA)
        merged = (x32 + jnp.dot(rows_a, conv_one, preferred_element_type=jnp.float32)).astype(jnp.bfloat16)
        grouped = merged.reshape(LB, 4 * CA)
        coarse = jnp.dot(grouped, down_proj, preferred_element_type=jnp.float32).astype(jnp.bfloat16)
        c32 = coarse.astype(jnp.float32)
        normed_b, factor_b = rms_fwd(c32)
        act_b = jax.nn.silu(normed_b).astype(jnp.bfloat16)
        rows_b = unfold(jnp.pad(act_b, ((1, 1), (0, 0))), LB)
        encoded = (c32 + jnp.dot(rows_b, conv_two, preferred_element_type=jnp.float32)).astype(jnp.bfloat16)
        contract = (((0,), (0,)), ((), ()))
        raw_two = lax.dot_general(rows_b, grad_out, contract, preferred_element_type=jnp.float32)
        back_b = conv_back(jnp.pad(grad_out, ((1, 1), (0, 0))), conv_two, LB)
        slope_b = back_b * silu_slope(normed_b)
        d_coarse = (grad_out.astype(jnp.float32) + rms_back(slope_b, normed_b, factor_b)).astype(jnp.bfloat16)
        raw_down = lax.dot_general(grouped, d_coarse, contract, preferred_element_type=jnp.float32)
        d_merged = lax.dot_general(d_coarse, down_proj, (((1,), (1,)), ((), ())), preferred_element_type=jnp.float32).reshape(LA, CA)
        d_hidden = d_merged.astype(jnp.bfloat16)
        raw_one = lax.dot_general(rows_a, d_hidden, contract, preferred_element_type=jnp.float32)
        back_a = conv_back(jnp.pad(d_hidden, ((1, 1), (0, 0))), conv_one, LA)
        d_pre = back_a * silu_slope(pre)
        dtemb = lax.optimization_barrier(jnp.sum(d_pre, axis=0))
        raw_time = emb_row[:, None] * dtemb[None, :]
        signal_grad = (d_merged + rms_back(d_pre, normed, factor)).astype(jnp.bfloat16)
        sums = (carry[0] + raw_one, carry[1] + raw_down, carry[2] + raw_two, carry[3] + raw_time)
        return (sums, (encoded, signal_grad))
    start = (jnp.zeros((3 * CA, CA), jnp.float32), jnp.zeros((4 * CA, CB), jnp.float32), jnp.zeros((3 * CB, CB), jnp.float32), jnp.zeros((EMB, CA), jnp.float32))
    sums, (encoded, signal_grad) = lax.scan(per_clip, start, (signal, emb_all, temb_all, cotangent))
    factor_all = 1.0 / math.sqrt(CLIPS * LA)
    return (encoded, signal_grad, sums[0] * factor_all, sums[1] * factor_all, sums[2] * factor_all, sums[3] * factor_all)
```

```python
import math

import jax
import jax.numpy as jnp
from jax import lax
from jax.experimental import pallas as pl
from jax.experimental.pallas import tpu as pltpu
from jax.sharding import PartitionSpec as P

EPS = 1e-06
CA, CB, EMB = 256, 512, 256
S = 512
E = 528
STEP = 176
F32, BF16 = jnp.float32, jnp.bfloat16
AXES = ("dp", "tm")
NT = (((1,), (1,)), ((), ()))


def dot(a, b):
    return jnp.dot(a, b, preferred_element_type=F32)


def dot_nt(a, b):
    return lax.dot_general(a, b, NT, preferred_element_type=F32)


def rows_of(i, size):
    return pl.ds(pl.multiple_of(i * size, 16), size)


def sigmoid(v):
    return 1.0 / (1.0 + jnp.exp(-v))


def inside(idx_ref, start, size, margin):
    row = lax.broadcasted_iota(jnp.int32, (size, 1), 0) + start
    past = jnp.logical_and(row >= S, row < S + margin)
    before = row >= E - margin
    off = jnp.logical_or(
        jnp.logical_and(past, idx_ref[4] == 1), jnp.logical_and(before, idx_ref[3] == 1)
    )
    return jnp.where(off, 0.0, 1.0)


def phase(ref, start, size):
    return jnp.concatenate([ref[h, pl.ds(start, size, stride=4), :] for h in range(2)], axis=1)


def later(v):
    return pltpu.roll(v, 1, 0)


def sooner(v):
    return pltpu.roll(v, v.shape[0] - 1, 0)


def grads_kernel(
    idx_ref, x_ref, left_ref, right_ref, cot_ref, temb_ref, one_ref, down_ref, two_ref,
    ga_ref, gb_ref, dc_ref, ab_ref, co_ref,
    xs_ref, uw_ref, mw_ref, ubw_ref, cw_ref, slope_ref, normed_ref, fac_ref, dh_ref,
):
    @pl.loop(0, 16)
    def _(i):
        r = rows_of(i, 128)
        v = x_ref[r, :].astype(F32)
        xs_ref[0, r, :] = v[:, :128]
        xs_ref[1, r, :] = v[:, 128:]

    for h in range(2):
        lanes = slice(h * 128, (h + 1) * 128)
        xs_ref[h, 2048:2056, :] = right_ref[:, lanes].astype(F32)
        xs_ref[h, 2056:2104, :] = jnp.zeros((48, 128), F32)
        xs_ref[h, 2104:2112, :] = left_ref[:, lanes].astype(F32)

    @pl.loop(0, 11)
    def _(i):
        r = rows_of(i, 48)
        keep = inside(idx_ref, i * 48, 48, 2)
        for j in range(4):
            v = phase(xs_ref, i * 192 + j, 48)
            pre = v * lax.rsqrt(jnp.mean(v * v, -1, keepdims=True) + EPS) + temb_ref[...]
            act = pre * sigmoid(pre) * keep
            uw_ref[r, (j + 1) * CA : (j + 2) * CA] = act.astype(BF16)

    uw_ref[:, :CA] = later(uw_ref[:, 4 * CA : 5 * CA].astype(F32)).astype(BF16)
    uw_ref[:, 5 * CA :] = sooner(uw_ref[:, CA : 2 * CA].astype(F32)).astype(BF16)

    zeros = jnp.zeros((12, CB), F32)
    cot = jnp.concatenate(
        [
            cot_ref[...].astype(F32),
            right_ref[:2, CA:].astype(F32),
            zeros,
            left_ref[6:, CA:].astype(F32),
        ],
        axis=0,
    )
    cw_ref[:, CB : 2 * CB] = cot.astype(BF16)
    cw_ref[:, :CB] = sooner(cot).astype(BF16)
    cw_ref[:, 2 * CB :] = later(cot).astype(BF16)

    @pl.loop(0, 3)
    def _(i):
        r = rows_of(i, STEP)
        for j in range(4):
            hidden = dot(uw_ref[r, j * CA : (j + 3) * CA], one_ref[...])
            v = phase(xs_ref, i * STEP * 4 + j, STEP)
            mw_ref[r, j * CA : (j + 1) * CA] = (v + hidden).astype(BF16)
        coarse = dot(mw_ref[r, :], down_ref[...]).astype(BF16)
        co_ref[r, :] = coarse
        c32 = coarse.astype(F32)
        factor = lax.rsqrt(jnp.mean(c32 * c32, -1, keepdims=True) + EPS)
        normed = c32 * factor
        sig = sigmoid(normed)
        keep = inside(idx_ref, i * STEP, STEP, 1)
        ubw_ref[r, CB : 2 * CB] = (normed * sig * keep).astype(BF16)
        fac_ref[r, :] = jnp.broadcast_to(factor, (STEP, 128))
        normed_ref[r, :] = normed
        slope_ref[r, :] = sig * (1.0 + normed * (1.0 - sig))

    act_b = ubw_ref[:, CB : 2 * CB]
    ab_ref[...] = act_b
    act_b = act_b.astype(F32)
    ubw_ref[:, :CB] = later(act_b).astype(BF16)
    ubw_ref[:, 2 * CB :] = sooner(act_b).astype(BF16)

    @pl.loop(0, 3)
    def _(i):
        r = rows_of(i, STEP)
        back = dot_nt(cw_ref[r, :CB], two_ref[:CB, :])
        back += dot_nt(cw_ref[r, CB : 2 * CB], two_ref[CB : 2 * CB, :])
        back += dot_nt(cw_ref[r, 2 * CB :], two_ref[2 * CB :, :])
        normed = normed_ref[r, :]
        q = back * slope_ref[r, :]
        m = jnp.mean(q * normed, -1, keepdims=True)
        keep = inside(idx_ref, i * STEP, STEP, 1)
        grad = cw_ref[r, CB : 2 * CB].astype(F32) + fac_ref[r, :1] * (q - normed * m)
        d_coarse = (grad * keep).astype(BF16)
        dc_ref[r, :] = d_coarse
        dh_ref[r, :] = dot_nt(d_coarse, down_ref[...]).astype(BF16)

    scaling = 1.0 / math.sqrt(16 * 32768)
    core, x, yhi = idx_ref[0], idx_ref[1], idx_ref[2]

    def place(chunk):
        c, xx, y = chunk % 2, (chunk // 2) % 4, chunk // 8
        return ((c + core) % 2) * 8 + ((xx + 4 - x) % 4) * 2 + (y + yhi) % 2

    def turned(ref, lanes):
        return ref[:S, lanes].astype(F32).T.astype(BF16)

    @pl.loop(0, 4)
    def _(i):
        lanes = pl.ds(pl.multiple_of(i * 128, 128), 128)
        at = cw_ref[:S, pl.ds(pl.multiple_of(CB + i * 128, 128), 128)].astype(F32).T.astype(BF16)
        two = (dot(at, ubw_ref[:S, :]) * scaling).astype(BF16)
        for c in range(4):
            ga_ref[place(i * 4 + c)] = two[c * 32 : (c + 1) * 32, :]
        at = turned(dc_ref, lanes)
        down = (dot(at, mw_ref[:S, :]) * scaling).astype(BF16)
        for c in range(4):
            gb_ref[place(i * 4 + c), :32] = down[c * 32 : (c + 1) * 32, :]

    @pl.loop(0, 2)
    def _(i):
        total = jnp.zeros((128, 3 * CA), F32)
        for j in range(4):
            lanes = pl.ds(pl.multiple_of(j * CA + i * 128, 128), 128)
            total += dot(turned(dh_ref, lanes), uw_ref[:S, j * CA : (j + 3) * CA])
        total = (total * scaling).astype(BF16)
        for c in range(8):
            gb_ref[place(i * 8 + c), 32:, : 3 * CA] = total[c * 16 : (c + 1) * 16, :]
            gb_ref[place(i * 8 + c), 32:, 3 * CA :] = jnp.zeros((16, EMB), BF16)


def outputs_kernel(
    x_ref, co_ref, ab_ref, dc_ref, temb_ref, one_ref, down_ref, two_ref,
    enc_ref, sg_ref, dt_ref,
    xs_ref, ys_ref, ubw_ref, dm_ref, dhw_ref,
):
    @pl.loop(0, 16)
    def _(i):
        r = rows_of(i, 128)
        v = x_ref[r, :].astype(F32)
        xs_ref[0, r, :] = v[:, :128]
        xs_ref[1, r, :] = v[:, 128:]

    act_b = ab_ref[...].astype(F32)
    ubw_ref[:, CB : 2 * CB] = ab_ref[...]
    ubw_ref[:, :CB] = later(act_b).astype(BF16)
    ubw_ref[:, 2 * CB :] = sooner(act_b).astype(BF16)

    @pl.loop(0, 4)
    def _(i):
        r = rows_of(i, 128)
        enc = co_ref[r, :].astype(F32) + dot(ubw_ref[r, :], two_ref[...])
        enc_ref[r, :] = enc.astype(BF16)

    @pl.loop(0, 3)
    def _(i):
        r = rows_of(i, STEP)
        dm = dot_nt(dc_ref[r, :], down_ref[...])
        dm_ref[r, :] = dm
        dhw_ref[r, CA : 5 * CA] = dm.astype(BF16)

    dhw_ref[:, :CA] = later(dhw_ref[:, 4 * CA : 5 * CA].astype(F32)).astype(BF16)
    dhw_ref[:, 5 * CA :] = sooner(dhw_ref[:, CA : 2 * CA].astype(F32)).astype(BF16)
    dt_ref[...] = jnp.zeros((8, CA), F32)

    @pl.loop(0, 4)
    def _(i):
        r = rows_of(i, 128)
        for j in range(4):
            back = dot_nt(dhw_ref[r, (j + 2) * CA : (j + 3) * CA], one_ref[:CA, :])
            back += dot_nt(dhw_ref[r, (j + 1) * CA : (j + 2) * CA], one_ref[CA : 2 * CA, :])
            back += dot_nt(dhw_ref[r, j * CA : (j + 1) * CA], one_ref[2 * CA :, :])
            v = phase(xs_ref, i * 512 + j, 128)
            factor = lax.rsqrt(jnp.mean(v * v, -1, keepdims=True) + EPS)
            normed = v * factor
            pre = normed + temb_ref[...]
            sig = sigmoid(pre)
            d_pre = back * (sig * (1.0 + pre * (1.0 - sig)))
            dt_ref[...] += d_pre.reshape(16, 8, CA).sum(0)
            m = jnp.mean(d_pre * normed, -1, keepdims=True)
            grad = dm_ref[r, j * CA : (j + 1) * CA] + factor * (d_pre - normed * m)
            ys_ref[0, pl.ds(i * 512 + j, 128, stride=4), :] = grad[:, :128]
            ys_ref[1, pl.ds(i * 512 + j, 128, stride=4), :] = grad[:, 128:]

    @pl.loop(0, 16)
    def _(i):
        r = rows_of(i, 128)
        sg_ref[r, :128] = ys_ref[0, r, :].astype(BF16)
        sg_ref[r, 128:] = ys_ref[1, r, :].astype(BF16)


def embed(stamps, width):
    half = width // 2
    freqs = jnp.exp(-math.log(10000.0) * jnp.arange(half, dtype=F32) / half)
    angles = stamps.astype(F32)[:, None] * freqs[None, :]
    return jnp.concatenate([jnp.sin(angles), jnp.cos(angles)], axis=-1)


def moved(value, target):
    pairs = [(i, target(i // 8, i // 2 % 4, i % 2)) for i in range(16)]
    return lax.ppermute(value, "tm", pairs)


def summed(first, *others):
    total = first.astype(F32)
    for other in others:
        total = total + other.astype(F32)
    return total.astype(BF16)


def pieces(value):
    return jnp.moveaxis(value.reshape(value.shape[0], 16, -1), 1, 0)


def per_device(signal, timesteps, cotangent, conv_one, down_proj, conv_two, time_proj):
    x, cot = signal[0], cotangent[0]
    forward = [(i, i + 1) for i in range(15)]
    backward = [(i + 1, i) for i in range(15)]
    left = lax.ppermute(jnp.concatenate([x[-8:], cot[-8:]], axis=1), "tm", forward)
    right = lax.ppermute(jnp.concatenate([x[:8], cot[:8]], axis=1), "tm", backward)
    emb_row = embed(timesteps, EMB)
    temb = jnp.dot(emb_row, time_proj.astype(F32), precision=lax.Precision.HIGHEST)
    tm = lax.axis_index("tm")
    idx = jnp.stack(
        [tm % 2, tm // 2 % 4, tm // 8, (tm == 0).astype(jnp.int32), (tm == 15).astype(jnp.int32)]
    ).astype(jnp.int32)
    smem = pl.BlockSpec(memory_space=pltpu.SMEM)
    vmem = pl.BlockSpec(memory_space=pltpu.VMEM)
    sds = jax.ShapeDtypeStruct
    ga, gb, dc, ab, co = pl.pallas_call(
        grads_kernel,
        name="grads",
        in_specs=[smem] + [vmem] * 8,
        out_specs=[vmem] * 5,
        out_shape=[
            sds((16, 32, 3 * CB), BF16),
            sds((16, 48, 4 * CA), BF16),
            sds((E, CB), BF16),
            sds((E, CB), BF16),
            sds((E, CB), BF16),
        ],
        scratch_shapes=[
            pltpu.VMEM((2, 4 * E, 128), F32),
            pltpu.VMEM((E, 6 * CA), BF16),
            pltpu.VMEM((E, 4 * CA), BF16),
            pltpu.VMEM((E, 3 * CB), BF16),
            pltpu.VMEM((E, 3 * CB), BF16),
            pltpu.VMEM((E, CB), F32),
            pltpu.VMEM((E, CB), F32),
            pltpu.VMEM((E, 128), F32),
            pltpu.VMEM((E, 4 * CA), BF16),
        ],
        cost_estimate=pl.CostEstimate(
            flops=4_900_000_000, bytes_accessed=10_000_000, transcendentals=1_600_000
        ),
        compiler_params=pltpu.CompilerParams(vmem_limit_bytes=48 << 20),
    )(idx, x, left, right, cot, temb, conv_one, down_proj, conv_two)

    def swap_core(v):
        return moved(v, lambda y, xx, c: y * 8 + xx * 2 + 1 - c)

    ra, rb = swap_core(ga[8:]), swap_core(gb[8:])
    encoded, signal_grad, dtemb = pl.pallas_call(
        outputs_kernel,
        name="outputs",
        in_specs=[vmem] * 8,
        out_specs=[vmem] * 3,
        out_shape=[sds((S, CB), BF16), sds((4 * S, CA), BF16), sds((8, CA), F32)],
        scratch_shapes=[
            pltpu.VMEM((2, 4 * S, 128), F32),
            pltpu.VMEM((2, 4 * S, 128), F32),
            pltpu.VMEM((E, 3 * CB), BF16),
            pltpu.VMEM((E, 4 * CA), F32),
            pltpu.VMEM((E, 6 * CA), BF16),
        ],
        cost_estimate=pl.CostEstimate(
            flops=2_150_000_000, bytes_accessed=7_000_000, transcendentals=600_000
        ),
        compiler_params=pltpu.CompilerParams(vmem_limit_bytes=48 << 20),
    )(x, co, ab, dc, temb, conv_one, down_proj, conv_two)

    def ring_x(v):
        return [
            moved(
                v[2 * k : 2 * k + 2], lambda y, xx, c, k=k: y * 8 + (xx + k) % 4 * 2 + c
            )
            for k in (1, 2, 3)
        ]

    def swap_y(v):
        return moved(v, lambda y, xx, c: (1 - y) * 8 + xx * 2 + c)

    ga, gb = summed(ga[:8], ra), summed(gb[:8], rb)
    ra, rb = ring_x(ga), ring_x(gb)
    ga, gb = summed(ga[:2], *ra), summed(gb[:2], *rb)
    ga, gb = summed(ga[0], swap_y(ga[1])), summed(gb[0], swap_y(gb[1]))

    scaling = 1.0 / math.sqrt(16 * 32768)
    cols = lax.all_to_all(dtemb.sum(0).reshape(16, 16), "tm", 0, 0, tiled=True).sum(0)
    time = (emb_row[0].reshape(16, 16)[:, None, :] * cols[None, :, None] * scaling).astype(BF16)

    two, down, one = pieces(ga), pieces(gb[:32]), pieces(gb[32:, : 3 * CA])
    lines = jnp.concatenate(
        [v.reshape(16, -1) for v in (two, down, one, time)], axis=1
    ).reshape(16, 48, 128)
    line = lax.all_to_all(lines, "dp", 0, 0, tiled=True).astype(F32).sum(0).reshape(-1)
    outs, at = [], 0
    for n, k in ((32, 96), (32, 64), (16, 48), (16, 16)):
        outs.append(line[at : at + n * k].reshape(n, k).T)
        at += n * k
    return encoded[None], signal_grad[None], outs[2], outs[1], outs[0], outs[3]


def solution(mesh):
    return jax.shard_map(
        per_device,
        mesh=mesh,
        in_specs=(P("dp", "tm", None), P("dp"), P("dp", "tm", None), P(), P(), P(), P()),
        out_specs=(
            P("dp", "tm", None),
            P("dp", "tm", None),
            P("dp", "tm"),
            P("dp", "tm"),
            P("dp", "tm"),
            P("dp", "tm"),
        ),
        check_vma=False,
    )
```

```python
import math

import jax
import jax.numpy as jnp
from jax import lax
from jax.experimental import pallas as pl
from jax.experimental.pallas import tpu as pltpu
from jax.sharding import PartitionSpec as P


EPS = 1e-06
CA, CB, EMB = 256, 512, 256
S = 512
E = 528
F32, BF16 = jnp.float32, jnp.bfloat16
AXES = ("dp", "tm")
NT = (((1,), (1,)), ((), ()))


def dot(a, b):
    return jnp.dot(a, b, preferred_element_type=F32)


def dot_nt(a, b):
    return lax.dot_general(a, b, NT, preferred_element_type=F32)


def rows_of(i, size):
    return pl.ds(pl.multiple_of(i * size, 16), size)


def sigmoid(v):
    return 1.0 / (1.0 + jnp.exp(-v))


def inside(idx_ref, start, size, margin):
    row = lax.broadcasted_iota(jnp.int32, (size, 1), 0) + start
    past = jnp.logical_and(row >= S, row < S + margin)
    before = row >= E - margin
    off = jnp.logical_or(
        jnp.logical_and(past, idx_ref[4] == 1), jnp.logical_and(before, idx_ref[3] == 1)
    )
    return jnp.where(off, 0.0, 1.0)


def phase(ref, start, size):
    return jnp.concatenate([ref[h, pl.ds(start, size, stride=4), :] for h in range(2)], axis=1)


def later(v):
    return pltpu.roll(v, 1, 0)


def sooner(v):
    return pltpu.roll(v, v.shape[0] - 1, 0)


def places(idx_ref, xx, y):
    apart = xx ^ idx_ref[1]
    side = y ^ idx_ref[2]
    first = jnp.where(apart == 3, 1, jnp.where(apart == 0, 0, apart + 1))
    second = jnp.where(apart < 2, apart, 5 - apart)
    return first * 2 + side, 8 + second * 2 + side


def put(idx_ref, keep_ref, send_ref, xx, y, rows, even, odd, at=0):
    core, half = idx_ref[0], keep_ref.shape[2]
    keep = jnp.where(core == 0, even, odd).astype(BF16)
    send = jnp.where(core == 0, odd, even).astype(BF16)
    for h, where in enumerate(places(idx_ref, xx, y)):
        low, high = max(at, h * half), min(at + even.shape[1], (h + 1) * half)
        if low < high:
            lanes = slice(low - h * half, high - h * half)
            keep_ref[where, rows, lanes] = keep[:, low - at : high - at]
            send_ref[where, rows, lanes] = send[:, low - at : high - at]


def rms(v):
    return lax.rsqrt(jnp.mean(v * v, -1, keepdims=True) + EPS)


def turned(v):
    return v.astype(F32).T.astype(BF16)


def edges_kernel(x_ref, cot_ref, first_ref, last_ref, sem):
    copies = []
    for out, at in ((first_ref, 0), (last_ref, 1)):
        n = len(copies)
        rows = (pl.ds(0, 8), pl.ds(4 * S - 8, 8))[at]
        copies.append(pltpu.make_async_copy(x_ref.at[rows, :], out.at[:, :CA], sem.at[n]))
        rows = (pl.ds(0, 8), pl.ds(S - 8, 8))[at]
        copies.append(pltpu.make_async_copy(cot_ref.at[rows, :], out.at[:, CA:], sem.at[n + 1]))
    for copy in copies:
        copy.start()
    for copy in copies:
        copy.wait()


def act_kernel(
    x_ref, cot_ref, one_ref, down_ref, temb_ref,
    xp_ref, act_ref, cot_out, one_out, down_out,
    xs_ref, xb_ref, sem,
):
    parts = []
    for k in range(4):
        rows = pl.ds(512 * k, 512)
        parts.append(pltpu.make_async_copy(x_ref.at[rows, :], xb_ref.at[rows, :], sem.at[k]))
    whole = [
        pltpu.make_async_copy(one_ref, one_out, sem.at[4]),
        pltpu.make_async_copy(cot_ref, cot_out, sem.at[5]),
        pltpu.make_async_copy(down_ref, down_out, sem.at[6]),
    ]
    for copy in parts + whole:
        copy.start()
    for k in range(4):
        parts[k].wait()

        @pl.loop(0, 2)
        def _(n):
            i = 2 * k + n
            r = rows_of(i, 256)
            v = xb_ref[r, :].astype(F32)
            xs_ref[0, r, :] = v[:, :128]
            xs_ref[1, r, :] = v[:, 128:]
            r = rows_of(i, 64)
            for j in range(4):
                v = phase(xs_ref, i * 256 + j, 64)
                pre = v * rms(v) + temb_ref[...]
                lanes = slice(j * CA, (j + 1) * CA)
                xp_ref[r, lanes] = v.astype(BF16)
                act_ref[r, lanes] = (pre * sigmoid(pre)).astype(BF16)

    for copy in whole:
        copy.wait()


def forward_kernel(
    idx_ref, xp_ref, act_ref, left_ref, right_ref, cot_ref, temb_ref, one_ref, down_ref,
    keep_ref, send_ref, mw_ref, uw_ref, ab_ref, co_ref,
    xs_ref, xe_ref, ubw_ref,
):
    for h in range(2):
        lanes = slice(h * 128, (h + 1) * 128)
        xs_ref[h, :8, :] = right_ref[:, lanes].astype(F32)
        xs_ref[h, 8:56, :] = jnp.zeros((48, 128), F32)
        xs_ref[h, 56:, :] = left_ref[:, lanes].astype(F32)
    inner = inside(idx_ref, S, E - S, 2)
    for j in range(4):
        v = phase(xs_ref, j, 16)
        pre = v * rms(v) + temb_ref[...]
        xe_ref[:, j * CA : (j + 1) * CA] = v
        uw_ref[S:, (j + 1) * CA : (j + 2) * CA] = (pre * sigmoid(pre) * inner).astype(BF16)
    uw_ref[:S, CA : 5 * CA] = act_ref[...]
    uw_ref[:, :CA] = later(uw_ref[:, 4 * CA : 5 * CA].astype(F32)).astype(BF16)
    uw_ref[:, 5 * CA :] = sooner(uw_ref[:, CA : 2 * CA].astype(F32)).astype(BF16)

    def block(r, size, start, x_of):
        for j in range(4):
            lanes = slice(j * CA, (j + 1) * CA)
            hidden = dot(uw_ref[r, j * CA : (j + 3) * CA], one_ref[...])
            mw_ref[r, lanes] = (x_of(lanes) + hidden).astype(BF16)
        coarse = dot(mw_ref[r, :], down_ref[...]).astype(BF16)
        co_ref[r, :] = coarse
        c32 = coarse.astype(F32)
        normed = c32 * rms(c32)
        keep = inside(idx_ref, start, size, 1)
        ubw_ref[r, CB : 2 * CB] = (normed * sigmoid(normed) * keep).astype(BF16)

    @pl.loop(0, 2)
    def _(i):
        r = rows_of(i, 256)
        block(r, 256, i * 256, lambda lanes: xp_ref[r, lanes].astype(F32))

    block(slice(S, E), E - S, S, lambda lanes: xe_ref[:, lanes])

    act_b = ubw_ref[:, CB : 2 * CB]
    ab_ref[...] = act_b
    act_b = act_b.astype(F32)
    ubw_ref[:, :CB] = later(act_b).astype(BF16)
    ubw_ref[:, 2 * CB :] = sooner(act_b).astype(BF16)

    scaling = 1.0 / math.sqrt(16 * 32768)

    @pl.loop(0, 4)
    def _(i):
        at = turned(cot_ref[:, pl.ds(pl.multiple_of(i * 128, 128), 128)])
        two = dot(at, ubw_ref[:S, :]) * scaling
        for c in range(2):
            even, odd = two[64 * c : 64 * c + 32], two[64 * c + 32 : 64 * c + 64]
            put(idx_ref, keep_ref, send_ref, (2 * i + c) % 4, i // 2, slice(None), even, odd)


def coarse_kernel(
    idx_ref, co_ref, cot_ref, left_ref, right_ref, down_ref, two_ref,
    dc_ref, dh_ref, dm_ref, cw_ref,
):
    cot = jnp.concatenate(
        [
            cot_ref[...].astype(F32),
            right_ref[:2, CA:].astype(F32),
            jnp.zeros((12, CB), F32),
            left_ref[6:, CA:].astype(F32),
        ],
        axis=0,
    )
    cw_ref[:, CB : 2 * CB] = cot.astype(BF16)
    cw_ref[:, :CB] = sooner(cot).astype(BF16)
    cw_ref[:, 2 * CB :] = later(cot).astype(BF16)

    def block(r, size, start):
        back = dot_nt(cw_ref[r, :CB], two_ref[:CB, :])
        back += dot_nt(cw_ref[r, CB : 2 * CB], two_ref[CB : 2 * CB, :])
        back += dot_nt(cw_ref[r, 2 * CB :], two_ref[2 * CB :, :])
        c32 = co_ref[r, :].astype(F32)
        factor = rms(c32)
        normed = c32 * factor
        sig = sigmoid(normed)
        q = back * (sig * (1.0 + normed * (1.0 - sig)))
        m = jnp.mean(q * normed, -1, keepdims=True)
        grad = cw_ref[r, CB : 2 * CB].astype(F32) + factor * (q - normed * m)
        d_coarse = (grad * inside(idx_ref, start, size, 1)).astype(BF16)
        dc_ref[r, :] = d_coarse
        return dot_nt(d_coarse, down_ref[...])

    @pl.loop(0, 2)
    def _(i):
        r = rows_of(i, 256)
        dm = block(r, 256, i * 256)
        dm_ref[r, :] = dm
        dh_ref[r, :] = dm.astype(BF16)

    dh_ref[S:, :] = block(slice(S, E), E - S, S).astype(BF16)


def fine_kernel(
    idx_ref, xp_ref, dc_ref, dh_ref, dm_ref, mw_ref, uw_ref, temb_ref, emb_ref, one_ref,
    keep_ref, send_ref, sg_ref,
    dhw_ref, ys_ref, dt_ref,
):
    scaling = 1.0 / math.sqrt(16 * 32768)
    dhw_ref[:, CA : 5 * CA] = dh_ref[...]
    dhw_ref[:, :CA] = later(dh_ref[:, 3 * CA :].astype(F32)).astype(BF16)
    dhw_ref[:, 5 * CA :] = sooner(dh_ref[:, :CA].astype(F32)).astype(BF16)
    dt_ref[...] = jnp.zeros((8, CA), F32)

    @pl.loop(0, 4)
    def _(i):
        r = rows_of(i, 128)
        for j in range(4):
            lanes = slice(j * CA, (j + 1) * CA)
            back = dot_nt(dhw_ref[r, (j + 2) * CA : (j + 3) * CA], one_ref[:CA, :])
            back += dot_nt(dhw_ref[r, (j + 1) * CA : (j + 2) * CA], one_ref[CA : 2 * CA, :])
            back += dot_nt(dhw_ref[r, lanes], one_ref[2 * CA :, :])
            v = xp_ref[r, lanes].astype(F32)
            factor = rms(v)
            normed = v * factor
            pre = normed + temb_ref[...]
            sig = sigmoid(pre)
            d_pre = back * (sig * (1.0 + pre * (1.0 - sig)))
            dt_ref[...] += d_pre.reshape(16, 8, CA).sum(0)
            m = jnp.mean(d_pre * normed, -1, keepdims=True)
            grad = dm_ref[r, lanes] + factor * (d_pre - normed * m)
            ys_ref[0, pl.ds(i * 512 + j, 128, stride=4), :] = grad[:, :128]
            ys_ref[1, pl.ds(i * 512 + j, 128, stride=4), :] = grad[:, 128:]

    @pl.loop(0, 16)
    def _(i):
        r = rows_of(i, 128)
        sg_ref[r, :128] = ys_ref[0, r, :].astype(BF16)
        sg_ref[r, 128:] = ys_ref[1, r, :].astype(BF16)

    @pl.loop(0, 4)
    def _(i):
        at = turned(dc_ref[:S, pl.ds(pl.multiple_of(i * 128, 128), 128)])
        down = dot(at, mw_ref[:S, :]) * scaling
        for c in range(2):
            even, odd = down[64 * c : 64 * c + 32], down[64 * c + 32 : 64 * c + 64]
            put(idx_ref, keep_ref, send_ref, (2 * i + c) % 4, i // 2, slice(0, 32), even, odd)

    dt = jnp.sum(dt_ref[...].T, axis=1, keepdims=True)
    for i in range(2):
        one = jnp.zeros((128, 3 * CA), F32)
        for j in range(4):
            at = turned(dh_ref[:S, j * CA + i * 128 : j * CA + (i + 1) * 128])
            one += dot(at, uw_ref[:S, j * CA : (j + 3) * CA])
        one *= scaling
        time = dt[i * 128 : (i + 1) * 128] * (emb_ref[...] * scaling)
        for xx in range(4):
            even, odd = slice(32 * xx, 32 * xx + 16), slice(32 * xx + 16, 32 * xx + 32)
            rows = slice(32, 48)
            put(idx_ref, keep_ref, send_ref, xx, i, rows, one[even], one[odd])
            put(idx_ref, keep_ref, send_ref, xx, i, rows, time[even], time[odd], 3 * CA)


def encoded_kernel(co_ref, ab_ref, two_ref, enc_ref, ubw_ref):
    act_b = ab_ref[...].astype(F32)
    ubw_ref[:, CB : 2 * CB] = ab_ref[...]
    ubw_ref[:, :CB] = later(act_b).astype(BF16)
    ubw_ref[:, 2 * CB :] = sooner(act_b).astype(BF16)

    @pl.loop(0, 2)
    def _(i):
        r = rows_of(i, 256)
        enc = co_ref[r, :].astype(F32) + dot(ubw_ref[r, :], two_ref[...])
        enc_ref[r, :] = enc.astype(BF16)


def add_kernel(terms, *refs):
    at = 0
    for out in refs[terms:]:
        rows = slice(at, at + out.shape[0])
        total = refs[0][rows].astype(F32)
        for ref in refs[1:terms]:
            total = total + ref[rows].astype(F32)
        out[...] = total.astype(BF16)
        at += out.shape[0]


def join_kernel(own_u, got_u, own_v, got_v, own_ref, send_ref):
    half = own_u.shape[2]
    for own, got, lanes in (
        (own_u, got_u, slice(0, half)),
        (own_v, got_v, slice(half, 2 * half)),
    ):
        own_ref[:, lanes] = (own[0].astype(F32) + got[0].astype(F32)).astype(BF16)
        send_ref[:, lanes] = (own[1].astype(F32) + got[1].astype(F32)).astype(BF16)


def lines_kernel(a_ref, a_got, b_ref, b_got, out_ref):
    two = a_ref[...].astype(F32) + a_got[...].astype(F32)
    rest = b_ref[...].astype(F32) + b_got[...].astype(F32)
    for d in range(16):
        down = rest[:32, 64 * d : 64 * d + 64]
        last = rest[32:, 48 * d : 48 * d + 48]
        time = rest[32:, 3 * CA + 16 * d : 3 * CA + 16 * d + 16]
        top = jnp.concatenate([two[:, 96 * d : 96 * d + 96], down[:, :32]], axis=1)
        low = jnp.concatenate([down[:16, 32:], down[16:, 32:], last, time], axis=1)
        out_ref[d] = jnp.concatenate([top, low], axis=0).astype(BF16)


def last_kernel(in_ref, one_ref, down_ref, two_ref, time_ref):
    line = in_ref[0].astype(F32)
    for d in range(1, 16):
        line = line + in_ref[d].astype(F32)
    two_ref[...] = line[:32, :96]
    down_ref[:, :32] = line[:32, 96:]
    down_ref[:16, 32:] = line[32:, :32]
    down_ref[16:, 32:] = line[32:, 32:64]
    one_ref[...] = line[32:, 64:112]
    time_ref[...] = line[32:, 112:].T


def call(kernel, operands, outs, scratch=(), flops=0, nbytes=0, smem=False, far=0, sems=0,
         room=24):
    vmem = pl.BlockSpec(memory_space=pltpu.VMEM)
    first = pl.BlockSpec(memory_space=pltpu.SMEM) if smem else vmem
    return pl.pallas_call(
        kernel,
        in_specs=[pl.BlockSpec(memory_space=pltpu.HBM)] * far
        + [vmem if far else first]
        + [vmem] * (len(operands) - far - 1)
        if far < len(operands)
        else [pl.BlockSpec(memory_space=pltpu.HBM)] * far,
        out_specs=[vmem] * len(outs),
        out_shape=[jax.ShapeDtypeStruct(shape, kind) for shape, kind in outs],
        scratch_shapes=[pltpu.VMEM(shape, kind) for shape, kind in scratch]
        + [pltpu.SemaphoreType.DMA((sems,))] * (sems > 0),
        cost_estimate=pl.CostEstimate(flops=flops, bytes_accessed=nbytes, transcendentals=0),
        compiler_params=pltpu.CompilerParams(vmem_limit_bytes=int(room * 2**20)),
    )(*operands)


def embed(stamps, width):
    half = width // 2
    freqs = jnp.exp(-math.log(10000.0) * jnp.arange(half, dtype=F32) / half)
    angles = stamps.astype(F32)[:, None] * freqs[None, :]
    return jnp.concatenate([jnp.sin(angles), jnp.cos(angles)], axis=-1)


def moved(value, target):
    pairs = [(i, target(i // 8, i // 2 % 4, i % 2)) for i in range(16)]
    return lax.ppermute(value, "tm", pairs)


def swap_core(v):
    return moved(v, lambda y, x, c: y * 8 + x * 2 + 1 - c)


def swap_x(v, apart):
    return moved(v, lambda y, x, c: y * 8 + (x ^ apart) * 2 + c)


def swap_y(v):
    pairs = [(i, i ^ (8 * 16 + 8)) for i in range(256)]
    return lax.ppermute(v, AXES, pairs)


def ring(parts):
    u, su, v, sv = parts
    gu = swap_x(su, 1)
    gv = swap_x(sv, 3)
    u, su = added([u, gu], (2, 2))
    v, sv = added([v, gv], (2, 2))
    gu = swap_x(su, 3)
    gv = swap_x(sv, 1)
    rows, half = u.shape[1:]
    own, send = call(
        join_kernel, [u, gu, v, gv], [((rows, 2 * half), BF16)] * 2,
        nbytes=600_000,
    )
    return own, swap_y(send)


def added(terms, cuts):
    tail = terms[0].shape[1:]
    size = math.prod(terms[0].shape) * 2
    return call(
        lambda *refs: add_kernel(len(terms), *refs), terms,
        [((n,) + tail, BF16) for n in cuts], nbytes=size * (len(terms) + 1),
    )


def per_device(signal, timesteps, cotangent, conv_one, down_proj, conv_two, time_proj):
    x, cot = signal[0], cotangent[0]
    forward = [(i, i + 1) for i in range(15)]
    backward = [(i + 1, i) for i in range(15)]
    first, last = call(
        edges_kernel, [x, cot], [((8, CA + CB), BF16)] * 2, nbytes=50_000, far=2, sems=4,
        room=60,
    )
    left = lax.ppermute(last, "tm", forward)
    right = lax.ppermute(first, "tm", backward)
    emb = embed(timesteps, EMB)
    temb = jnp.dot(emb, time_proj.astype(F32), precision=lax.Precision.HIGHEST)
    tm = lax.axis_index("tm")
    idx = jnp.stack(
        [tm & 1, (tm >> 1) & 3, tm >> 3, (tm == 0).astype(jnp.int32), (tm == 15).astype(jnp.int32)]
    ).astype(jnp.int32)

    xp, act, cot, conv_one, down_proj = call(
        act_kernel, [x, cot, conv_one, down_proj, temb],
        [((S, 4 * CA), BF16)] * 2
        + [(v.shape, BF16) for v in (cot, conv_one, down_proj)],
        [((2, 4 * S, 128), F32), ((4 * S, CA), BF16)], 50_000_000, 6_500_000, far=4, sems=7,
        room=48,
    )
    a_keep, a_send, mw, uw, ab, co = call(
        forward_kernel,
        [idx, xp, act, left, right, cot, temb, conv_one, down_proj],
        [((16, 32, 3 * CB // 2), BF16)] * 2
        + [((E, 4 * CA), BF16), ((E, 6 * CA), BF16), ((E, CB), BF16), ((E, CB), BF16)],
        [((2, 64, 128), F32), ((E - S, 4 * CA), F32), ((E, 3 * CB), BF16)],
        2_200_000_000, 10_000_000, smem=True,
    )
    a_got = swap_core(a_send)
    dc, dh, dm = call(
        coarse_kernel, [idx, co, cot, left, right, down_proj, conv_two],
        [((E, CB), BF16), ((E, 4 * CA), BF16), ((S, 4 * CA), F32)],
        [((E, 3 * CB), BF16)], 1_400_000_000, 7_000_000, smem=True,
    )
    a_parts = added([a_keep, a_got], (4, 4, 4, 4))
    a_own, a_got = ring(a_parts)
    b_keep, b_send, signal_grad = call(
        fine_kernel, [idx, xp, dc, dh, dm, mw, uw, temb, emb, conv_one],
        [((16, 48, 2 * CA), BF16)] * 2 + [((4 * S, CA), BF16)],
        [((E, 6 * CA), BF16), ((2, 4 * S, 128), F32), ((8, CA), F32)],
        2_200_000_000, 11_000_000, smem=True,
    )
    b_got = swap_core(b_send)
    (encoded,) = call(
        encoded_kernel, [co, ab, conv_two], [((S, CB), BF16)],
        [((E, 3 * CB), BF16)], 800_000_000, 3_000_000,
    )
    b_parts = added([b_keep, b_got], (4, 4, 4, 4))
    b_own, b_got = ring(b_parts)
    (lines,) = call(
        lines_kernel, [a_own, a_got, b_own, b_got],
        [((16, 48, 128), BF16)], nbytes=900_000,
    )
    lines = lax.all_to_all(lines, "dp", 0, 0, tiled=True)
    outs = call(
        last_kernel, [lines],
        [((16, 48), F32), ((32, 64), F32), ((32, 96), F32), ((16, 16), F32)], nbytes=300_000,
    )
    one, down, two, time = outs
    return encoded[None], signal_grad[None], one.T, down.T, two.T, time


def solution(mesh):
    return jax.shard_map(
        per_device,
        mesh=mesh,
        in_specs=(P("dp", "tm", None), P("dp"), P("dp", "tm", None), P(), P(), P(), P()),
        out_specs=(
            P("dp", "tm", None),
            P("dp", "tm", None),
            P("dp", "tm"),
            P("dp", "tm"),
            P("dp", "tm"),
            P("dp", "tm"),
        ),
        check_vma=False,
    )
```

```python
import math

import jax
import jax.numpy as jnp
from jax import lax
from jax.experimental import pallas as pl
from jax.experimental.pallas import tpu as pltpu
from jax.sharding import PartitionSpec as P


EPS = 1e-06
CA, CB, EMB = 256, 512, 256
S = 512
E = 528
STEP = 176
F32, BF16 = jnp.float32, jnp.bfloat16
AXES = ("dp", "tm")
NT = (((1,), (1,)), ((), ()))


def dot(a, b):
    return jnp.dot(a, b, preferred_element_type=F32)


def dot_nt(a, b):
    return lax.dot_general(a, b, NT, preferred_element_type=F32)


def rows_of(i, size):
    return pl.ds(pl.multiple_of(i * size, 16), size)


def sigmoid(v):
    return 0.5 * jnp.tanh(0.5 * v) + 0.5


def inside(idx_ref, start, size, margin):
    row = lax.broadcasted_iota(jnp.int32, (size, 1), 0) + start
    past = jnp.logical_and(row >= S, row < S + margin)
    before = row >= E - margin
    off = jnp.logical_or(
        jnp.logical_and(past, idx_ref[4] == 1), jnp.logical_and(before, idx_ref[3] == 1)
    )
    return jnp.where(off, 0.0, 1.0)


def phase(ref, start, size):
    return jnp.concatenate([ref[h, pl.ds(start, size, stride=4), :] for h in range(2)], axis=1)


def later(v):
    return pltpu.roll(v, 1, 0)


def sooner(v):
    return pltpu.roll(v, v.shape[0] - 1, 0)


def places(idx_ref, xx, y):
    apart = xx ^ idx_ref[1]
    side = y ^ idx_ref[2]
    first = jnp.where(apart == 3, 1, jnp.where(apart == 0, 0, apart + 1))
    second = jnp.where(apart < 2, apart, 5 - apart)
    return first * 2 + side, 8 + second * 2 + side


def put(idx_ref, keep_ref, send_ref, xx, y, rows, even, odd, at=0):
    core, half = idx_ref[0], keep_ref.shape[2]
    keep = jnp.where(core == 0, even, odd).astype(BF16)
    send = jnp.where(core == 0, odd, even).astype(BF16)
    for h, where in enumerate(places(idx_ref, xx, y)):
        low, high = max(at, h * half), min(at + even.shape[1], (h + 1) * half)
        if low < high:
            lanes = slice(low - h * half, high - h * half)
            keep_ref[where, rows, lanes] = keep[:, low - at : high - at]
            send_ref[where, rows, lanes] = send[:, low - at : high - at]


def rms(v):
    return lax.rsqrt(jnp.mean(v * v, -1, keepdims=True) + EPS)


def turned(v):
    return v.astype(F32).T.astype(BF16)


def edges_kernel(idx_ref, x_ref, cot_ref, one_ref, two_ref, sem):
    copies = []
    for n, out in enumerate((one_ref, two_ref)):
        last = idx_ref[0] ^ n
        rows = pl.ds(pl.multiple_of(last * (4 * S - 8), 8), 8)
        copies.append(pltpu.make_async_copy(x_ref.at[rows, :], out.at[:, :CA], sem.at[2 * n]))
        rows = pl.ds(pl.multiple_of(last * (S - 8), 8), 8)
        copies.append(
            pltpu.make_async_copy(cot_ref.at[rows, :], out.at[:, CA:], sem.at[2 * n + 1])
        )
    for copy in copies:
        copy.start()
    for copy in copies:
        copy.wait()


def sides(idx_ref, chip_ref, core_ref, rows, lanes):
    chip = chip_ref[:, lanes].astype(F32)
    core = core_ref[:, lanes].astype(F32)
    even = idx_ref[0] == 0
    before, behind = jnp.where(even, chip, core), jnp.where(even, core, chip)
    return before[8 - rows :], behind[:rows]


def act_kernel(
    x_ref, cot_ref, one_ref, down_ref, temb_ref,
    xp_ref, act_ref, cot_out, one_out, down_out,
    xs_ref, xb_ref, sem,
):
    parts = []
    for k in range(4):
        rows = pl.ds(512 * k, 512)
        parts.append(pltpu.make_async_copy(x_ref.at[rows, :], xb_ref.at[rows, :], sem.at[k]))
    whole = [
        pltpu.make_async_copy(one_ref, one_out, sem.at[4]),
        pltpu.make_async_copy(cot_ref, cot_out, sem.at[5]),
        pltpu.make_async_copy(down_ref, down_out, sem.at[6]),
    ]
    for copy in parts + whole:
        copy.start()
    for k in range(4):
        parts[k].wait()

        @pl.loop(0, 2)
        def _(n):
            i = 2 * k + n
            r = rows_of(i, 256)
            v = xb_ref[r, :].astype(F32)
            xs_ref[0, r, :] = v[:, :128]
            xs_ref[1, r, :] = v[:, 128:]
            r = rows_of(i, 64)
            for j in range(4):
                v = phase(xs_ref, i * 256 + j, 64)
                pre = v * rms(v) + temb_ref[...]
                lanes = slice(j * CA, (j + 1) * CA)
                xp_ref[r, lanes] = v.astype(BF16)
                act_ref[r, lanes] = (pre * sigmoid(pre)).astype(BF16)

    for copy in whole:
        copy.wait()


def forward_kernel(
    idx_ref, xp_ref, act_ref, chip_ref, core_ref, cot_ref, temb_ref, one_ref, down_ref,
    keep_ref, send_ref, mw_ref, uw_ref, ab_ref, co_ref,
    xs_ref, ubw_ref, at_ref,
):
    before, behind = sides(idx_ref, chip_ref, core_ref, 8, slice(0, CA))
    for h in range(2):
        lanes = slice(h * 128, (h + 1) * 128)
        xs_ref[h, :8, :] = behind[:, lanes]
        xs_ref[h, 8:56, :] = jnp.zeros((48, 128), F32)
        xs_ref[h, 56:, :] = before[:, lanes]
    inner = inside(idx_ref, S, E - S, 2)
    for j in range(4):
        v = phase(xs_ref, j, 16)
        pre = v * rms(v) + temb_ref[...]
        uw_ref[S:, (j + 1) * CA : (j + 2) * CA] = (pre * sigmoid(pre) * inner).astype(BF16)
    uw_ref[:S, CA : 5 * CA] = act_ref[...]
    uw_ref[:, :CA] = later(uw_ref[:, 4 * CA : 5 * CA].astype(F32)).astype(BF16)
    uw_ref[:, 5 * CA :] = sooner(uw_ref[:, CA : 2 * CA].astype(F32)).astype(BF16)
    for i in range(4):
        lanes = slice(i * 128, (i + 1) * 128)
        at_ref[lanes, :] = turned(cot_ref[:, lanes])

    for j in range(4):
        lanes = slice(j * CA, (j + 1) * CA)
        hidden = dot(uw_ref[:, j * CA : (j + 3) * CA], one_ref[...])
        mw_ref[:S, lanes] = (xp_ref[:, lanes].astype(F32) + hidden[:S]).astype(BF16)
        mw_ref[S:, lanes] = (phase(xs_ref, j, 16) + hidden[S:]).astype(BF16)
    for n in range(2):
        lanes = slice(n * CA, (n + 1) * CA)
        co_ref[:, lanes] = dot(mw_ref[...], down_ref[:, lanes]).astype(BF16)

    @pl.loop(0, 3)
    def _(i):
        r = rows_of(i, STEP)
        c32 = co_ref[r, :].astype(F32)
        normed = c32 * rms(c32)
        keep = inside(idx_ref, i * STEP, STEP, 1)
        ubw_ref[r, CB : 2 * CB] = (normed * sigmoid(normed) * keep).astype(BF16)

    act_b = ubw_ref[:, CB : 2 * CB]
    ab_ref[...] = act_b
    act_b = act_b.astype(F32)
    ubw_ref[:, :CB] = later(act_b).astype(BF16)
    ubw_ref[:, 2 * CB :] = sooner(act_b).astype(BF16)

    scaling = 1.0 / math.sqrt(16 * 32768)
    for n in range(6):
        two = dot(at_ref[...], ubw_ref[:S, n * CA : (n + 1) * CA]) * scaling
        for c in range(8):
            even, odd = two[64 * c : 64 * c + 32], two[64 * c + 32 : 64 * c + 64]
            put(idx_ref, keep_ref, send_ref, c % 4, c // 4, slice(None), even, odd, n * CA)


def coarse_kernel(
    idx_ref, co_ref, cot_ref, chip_ref, core_ref, down_ref, two_ref,
    dc_ref, dh_ref, dm_ref,
    cw_ref, back_ref,
):
    before, behind = sides(idx_ref, chip_ref, core_ref, 2, slice(CA, None))
    cot = jnp.concatenate(
        [cot_ref[...].astype(F32), behind, jnp.zeros((12, CB), F32), before], axis=0
    )
    cw_ref[:, CB : 2 * CB] = cot.astype(BF16)
    cw_ref[:, :CB] = sooner(cot).astype(BF16)
    cw_ref[:, 2 * CB :] = later(cot).astype(BF16)
    for n in range(2):
        lanes = slice(n * CA, (n + 1) * CA)
        back = dot_nt(cw_ref[:, :CB], two_ref[n * CA : (n + 1) * CA, :])
        back += dot_nt(cw_ref[:, CB : 2 * CB], two_ref[CB + n * CA : CB + (n + 1) * CA, :])
        back += dot_nt(cw_ref[:, 2 * CB :], two_ref[2 * CB + n * CA : 2 * CB + (n + 1) * CA, :])
        back_ref[:, lanes] = back

    @pl.loop(0, 3)
    def _(i):
        r = rows_of(i, STEP)
        c32 = co_ref[r, :].astype(F32)
        factor = rms(c32)
        normed = c32 * factor
        sig = sigmoid(normed)
        q = back_ref[r, :] * (sig * (1.0 + normed * (1.0 - sig)))
        m = jnp.mean(q * normed, -1, keepdims=True)
        grad = cw_ref[r, CB : 2 * CB].astype(F32) + factor * (q - normed * m)
        dc_ref[r, :] = (grad * inside(idx_ref, i * STEP, STEP, 1)).astype(BF16)

    for n in range(4):
        lanes = slice(n * CA, (n + 1) * CA)
        dm = dot_nt(dc_ref[...], down_ref[lanes, :])
        dm_ref[:, lanes] = dm[:S]
        dh_ref[:, lanes] = dm.astype(BF16)


def fine_kernel(
    idx_ref, xp_ref, dc_ref, dh_ref, dm_ref, mw_ref, uw_ref, temb_ref, emb_ref, one_ref,
    keep_ref, send_ref, sg_ref,
    dhw_ref, ys_ref, dt_ref, at_ref, dt_all_ref,
):
    scaling = 1.0 / math.sqrt(16 * 32768)
    dhw_ref[:, CA : 5 * CA] = dh_ref[...]
    dhw_ref[:, :CA] = later(dh_ref[:, 3 * CA :].astype(F32)).astype(BF16)
    dhw_ref[:, 5 * CA :] = sooner(dh_ref[:, :CA].astype(F32)).astype(BF16)
    dt_ref[...] = jnp.zeros((8, CA), F32)
    for i in range(4):
        lanes = slice(i * 128, (i + 1) * 128)
        at_ref[lanes, :] = turned(dc_ref[:S, lanes])
    for j in range(4):
        for i in range(2):
            lanes = slice(j * CA + i * 128, j * CA + (i + 1) * 128)
            dt_all_ref[i * 128 : (i + 1) * 128, j * S : (j + 1) * S] = turned(dh_ref[:S, lanes])

    @pl.loop(0, 2)
    def _(i):
        r = rows_of(i, 256)
        for j in range(4):
            lanes = slice(j * CA, (j + 1) * CA)
            back = dot_nt(dhw_ref[r, (j + 2) * CA : (j + 3) * CA], one_ref[:CA, :])
            back += dot_nt(dhw_ref[r, (j + 1) * CA : (j + 2) * CA], one_ref[CA : 2 * CA, :])
            back += dot_nt(dhw_ref[r, lanes], one_ref[2 * CA :, :])
            v = xp_ref[r, lanes].astype(F32)
            factor = rms(v)
            normed = v * factor
            pre = normed + temb_ref[...]
            sig = sigmoid(pre)
            d_pre = back * (sig * (1.0 + pre * (1.0 - sig)))
            dt_ref[...] += d_pre.reshape(32, 8, CA).sum(0)
            m = jnp.mean(d_pre * normed, -1, keepdims=True)
            grad = dm_ref[r, lanes] + factor * (d_pre - normed * m)
            ys_ref[0, pl.ds(i * 1024 + j, 256, stride=4), :] = grad[:, :128]
            ys_ref[1, pl.ds(i * 1024 + j, 256, stride=4), :] = grad[:, 128:]

    @pl.loop(0, 16)
    def _(i):
        r = rows_of(i, 128)
        sg_ref[r, :128] = ys_ref[0, r, :].astype(BF16)
        sg_ref[r, 128:] = ys_ref[1, r, :].astype(BF16)

    for n in range(4):
        down = dot(at_ref[...], mw_ref[:S, n * CA : (n + 1) * CA]) * scaling
        for c in range(8):
            even, odd = down[64 * c : 64 * c + 32], down[64 * c + 32 : 64 * c + 64]
            put(idx_ref, keep_ref, send_ref, c % 4, c // 4, slice(0, 32), even, odd, n * CA)

    for n in range(4):
        if n < 3:
            one = jnp.zeros((CA, CA), F32)
            for j in range(4):
                lanes = slice((j + n) * CA, (j + n + 1) * CA)
                one += dot(dt_all_ref[:, j * S : (j + 1) * S], uw_ref[:S, lanes])
            one *= scaling
        else:
            dt = jnp.sum(dt_ref[...].T, axis=1, keepdims=True)
            one = dt * (emb_ref[...] * scaling)
        for c in range(8):
            even, odd = one[32 * c : 32 * c + 16], one[32 * c + 16 : 32 * c + 32]
            put(idx_ref, keep_ref, send_ref, c % 4, c // 4, slice(32, 48), even, odd, n * CA)


def encoded_kernel(co_ref, ab_ref, two_ref, enc_ref, ubw_ref):
    act_b = ab_ref[...].astype(F32)
    ubw_ref[:, CB : 2 * CB] = ab_ref[...]
    ubw_ref[:, :CB] = later(act_b).astype(BF16)
    ubw_ref[:, 2 * CB :] = sooner(act_b).astype(BF16)

    for n in range(2):
        lanes = slice(n * CA, (n + 1) * CA)
        enc = co_ref[:S, lanes].astype(F32) + dot(ubw_ref[:S, :], two_ref[:, lanes])
        enc_ref[:, lanes] = enc.astype(BF16)


def add_kernel(terms, *refs):
    at = 0
    for out in refs[terms:]:
        rows = slice(at, at + out.shape[0])
        total = refs[0][rows].astype(F32)
        for ref in refs[1:terms]:
            total = total + ref[rows].astype(F32)
        out[...] = total.astype(BF16)
        at += out.shape[0]


def join_kernel(own_u, got_u, own_v, got_v, own_ref, send_ref):
    half = own_u.shape[2]
    for own, got, lanes in (
        (own_u, got_u, slice(0, half)),
        (own_v, got_v, slice(half, 2 * half)),
    ):
        own_ref[:, lanes] = (own[0].astype(F32) + got[0].astype(F32)).astype(BF16)
        send_ref[:, lanes] = (own[1].astype(F32) + got[1].astype(F32)).astype(BF16)


def lines_kernel(a_ref, a_got, b_ref, b_got, out_ref):
    two = a_ref[...].astype(F32) + a_got[...].astype(F32)
    rest = b_ref[...].astype(F32) + b_got[...].astype(F32)
    for d in range(16):
        down = rest[:32, 64 * d : 64 * d + 64]
        last = rest[32:, 48 * d : 48 * d + 48]
        time = rest[32:, 3 * CA + 16 * d : 3 * CA + 16 * d + 16]
        top = jnp.concatenate([two[:, 96 * d : 96 * d + 96], down[:, :32]], axis=1)
        low = jnp.concatenate([down[:16, 32:], down[16:, 32:], last, time], axis=1)
        out_ref[d] = jnp.concatenate([top, low], axis=0).astype(BF16)


def last_kernel(in_ref, one_ref, down_ref, two_ref, time_ref):
    line = in_ref[0].astype(F32)
    for d in range(1, 16):
        line = line + in_ref[d].astype(F32)
    two_ref[...] = line[:32, :96]
    down_ref[:, :32] = line[:32, 96:]
    down_ref[:16, 32:] = line[32:, :32]
    down_ref[16:, 32:] = line[32:, 32:64]
    one_ref[...] = line[32:, 64:112]
    time_ref[...] = line[32:, 112:].T


def call(kernel, operands, outs, scratch=(), flops=0, nbytes=0, smem=False, far=0, sems=0,
         room=24):
    vmem = pl.BlockSpec(memory_space=pltpu.VMEM)
    return pl.pallas_call(
        kernel,
        in_specs=[pl.BlockSpec(memory_space=pltpu.SMEM)] * smem
        + [pl.BlockSpec(memory_space=pltpu.HBM)] * far
        + [vmem] * (len(operands) - far - smem),
        out_specs=[vmem] * len(outs),
        out_shape=[jax.ShapeDtypeStruct(shape, kind) for shape, kind in outs],
        scratch_shapes=[pltpu.VMEM(shape, kind) for shape, kind in scratch]
        + [pltpu.SemaphoreType.DMA((sems,))] * (sems > 0),
        cost_estimate=pl.CostEstimate(flops=flops, bytes_accessed=nbytes, transcendentals=0),
        compiler_params=pltpu.CompilerParams(vmem_limit_bytes=int(room * 2**20)),
    )(*operands)


def embed(stamps, width):
    half = width // 2
    freqs = jnp.exp(-math.log(10000.0) * jnp.arange(half, dtype=F32) / half)
    angles = stamps.astype(F32)[:, None] * freqs[None, :]
    return jnp.concatenate([jnp.sin(angles), jnp.cos(angles)], axis=-1)


def moved(value, target):
    pairs = [(i, target(i // 8, i // 2 % 4, i % 2)) for i in range(16)]
    return lax.ppermute(value, "tm", pairs)


def swap_core(v):
    return moved(v, lambda y, x, c: y * 8 + x * 2 + 1 - c)


def swap_x(v, apart):
    return moved(v, lambda y, x, c: y * 8 + (x ^ apart) * 2 + c)


def swap_y(v):
    pairs = [(i, i ^ (8 * 16 + 8)) for i in range(256)]
    return lax.ppermute(v, AXES, pairs)


def ring(parts):
    u, su, v, sv = parts
    gu = swap_x(su, 1)
    gv = swap_x(sv, 3)
    u, su = added([u, gu], (2, 2))
    v, sv = added([v, gv], (2, 2))
    gu = swap_x(su, 3)
    gv = swap_x(sv, 1)
    rows, half = u.shape[1:]
    own, send = call(
        join_kernel, [u, gu, v, gv], [((rows, 2 * half), BF16)] * 2,
        nbytes=600_000,
    )
    return own, swap_y(send)


def added(terms, cuts):
    tail = terms[0].shape[1:]
    size = math.prod(terms[0].shape) * 2
    return call(
        lambda *refs: add_kernel(len(terms), *refs), terms,
        [((n,) + tail, BF16) for n in cuts], nbytes=size * (len(terms) + 1),
    )


def per_device(signal, timesteps, cotangent, conv_one, down_proj, conv_two, time_proj):
    x, cot = signal[0], cotangent[0]
    tm = lax.axis_index("tm")
    idx = jnp.stack(
        [tm & 1, (tm >> 1) & 3, tm >> 3, (tm == 0).astype(jnp.int32), (tm == 15).astype(jnp.int32)]
    ).astype(jnp.int32)
    for_chip, for_core = call(
        edges_kernel, [idx, x, cot], [((8, CA + CB), BF16)] * 2, nbytes=50_000,
        smem=True, far=2, sems=4, room=60,
    )
    chip = lax.ppermute(for_chip, "tm", [(i, i + 1 if i % 2 else i - 1) for i in range(1, 15)])
    core = lax.ppermute(for_core, "tm", [(i, i ^ 1) for i in range(16)])
    emb = embed(timesteps, EMB)
    temb = jnp.dot(emb, time_proj.astype(F32), precision=lax.Precision.HIGHEST)
    xp, act, cot, conv_one, down_proj = call(
        act_kernel, [x, cot, conv_one, down_proj, temb],
        [((S, 4 * CA), BF16)] * 2
        + [(v.shape, BF16) for v in (cot, conv_one, down_proj)],
        [((2, 4 * S, 128), F32), ((4 * S, CA), BF16)], 50_000_000, 6_500_000, far=4, sems=7,
        room=48,
    )
    a_keep, a_send, mw, uw, ab, co = call(
        forward_kernel,
        [idx, xp, act, chip, core, cot, temb, conv_one, down_proj],
        [((16, 32, 3 * CB // 2), BF16)] * 2
        + [((E, 4 * CA), BF16), ((E, 6 * CA), BF16), ((E, CB), BF16), ((E, CB), BF16)],
        [((2, 64, 128), F32), ((E, 3 * CB), BF16), ((CB, S), BF16)],
        2_200_000_000, 10_000_000, smem=True,
    )
    a_got = swap_core(a_send)
    dc, dh, dm = call(
        coarse_kernel, [idx, co, cot, chip, core, down_proj, conv_two],
        [((E, CB), BF16), ((E, 4 * CA), BF16), ((S, 4 * CA), F32)],
        [((E, 3 * CB), BF16), ((E, CB), F32)], 1_400_000_000, 7_000_000, smem=True,
    )
    a_parts = added([a_keep, a_got], (4, 4, 4, 4))
    a_own, a_got = ring(a_parts)
    b_keep, b_send, signal_grad = call(
        fine_kernel, [idx, xp, dc, dh, dm, mw, uw, temb, emb, conv_one],
        [((16, 48, 2 * CA), BF16)] * 2 + [((4 * S, CA), BF16)],
        [
            ((E, 6 * CA), BF16), ((2, 4 * S, 128), F32), ((8, CA), F32), ((CB, S), BF16),
            ((CA, 4 * S), BF16),
        ],
        2_200_000_000, 11_000_000, smem=True,
    )
    b_got = swap_core(b_send)
    (encoded,) = call(
        encoded_kernel, [co, ab, conv_two], [((S, CB), BF16)],
        [((E, 3 * CB), BF16)], 800_000_000, 3_000_000,
    )
    b_parts = added([b_keep, b_got], (4, 4, 4, 4))
    b_own, b_got = ring(b_parts)
    (lines,) = call(
        lines_kernel, [a_own, a_got, b_own, b_got],
        [((16, 48, 128), BF16)], nbytes=900_000,
    )
    lines = lax.all_to_all(lines, "dp", 0, 0, tiled=True)
    outs = call(
        last_kernel, [lines],
        [((16, 48), F32), ((32, 64), F32), ((32, 96), F32), ((16, 16), F32)], nbytes=300_000,
    )
    one, down, two, time = outs
    return encoded[None], signal_grad[None], one.T, down.T, two.T, time


def solution(mesh):
    return jax.shard_map(
        per_device,
        mesh=mesh,
        in_specs=(P("dp", "tm", None), P("dp"), P("dp", "tm", None), P(), P(), P(), P()),
        out_specs=(
            P("dp", "tm", None),
            P("dp", "tm", None),
            P("dp", "tm"),
            P("dp", "tm"),
            P("dp", "tm"),
            P("dp", "tm"),
        ),
        check_vma=False,
    )
```

```python
import math

import jax
import jax.numpy as jnp
from jax import lax
from jax.experimental import pallas as pl
from jax.experimental.pallas import tpu as pltpu
from jax.sharding import PartitionSpec as P


EPS = 1e-06
CA, CB, EMB = 256, 512, 256
S = 512
E = 528
STEP = 176
F32, BF16 = jnp.float32, jnp.bfloat16
AXES = ("dp", "tm")
NT = (((1,), (1,)), ((), ()))


def dot(a, b):
    return jnp.dot(a, b, preferred_element_type=F32)


def dot_nt(a, b):
    return lax.dot_general(a, b, NT, preferred_element_type=F32)


def rows_of(i, size):
    return pl.ds(pl.multiple_of(i * size, 16), size)


def sigmoid(v):
    return 0.5 * jnp.tanh(0.5 * v) + 0.5


def inside(idx_ref, start, size, margin):
    row = lax.broadcasted_iota(jnp.int32, (size, 1), 0) + start
    past = jnp.logical_and(row >= S, row < S + margin)
    before = row >= E - margin
    off = jnp.logical_or(
        jnp.logical_and(past, idx_ref[0] == 15), jnp.logical_and(before, idx_ref[0] == 0)
    )
    return jnp.where(off, 0.0, 1.0)


def phase(ref, start, size):
    return jnp.concatenate([ref[h, pl.ds(start, size, stride=4), :] for h in range(2)], axis=1)


def later(v):
    return pltpu.roll(v, 1, 0)


def sooner(v):
    return pltpu.roll(v, v.shape[0] - 1, 0)


def places(idx_ref, xx, y):
    apart = xx ^ ((idx_ref[0] >> 1) & 3)
    side = y ^ (idx_ref[0] >> 3)
    first = jnp.where(apart == 3, 1, jnp.where(apart == 0, 0, apart + 1))
    second = jnp.where(apart < 2, apart, 5 - apart)
    return first * 2 + side, 8 + second * 2 + side


def put(idx_ref, keep_ref, send_ref, xx, y, rows, even, odd, at=0):
    core, half = idx_ref[0] & 1, keep_ref.shape[2]
    keep = jnp.where(core == 0, even, odd).astype(BF16)
    send = jnp.where(core == 0, odd, even).astype(BF16)
    for h, where in enumerate(places(idx_ref, xx, y)):
        low, high = max(at, h * half), min(at + even.shape[1], (h + 1) * half)
        if low < high:
            lanes = slice(low - h * half, high - h * half)
            keep_ref[where, rows, lanes] = keep[:, low - at : high - at]
            send_ref[where, rows, lanes] = send[:, low - at : high - at]


def rms(v):
    return lax.rsqrt(jnp.mean(v * v, -1, keepdims=True) + EPS)


def turned(v):
    return v.astype(F32).T.astype(BF16)


def edges_kernel(idx_ref, x_ref, cot_ref, one_ref, two_ref, sem):
    copies = []
    for n, out in enumerate((one_ref, two_ref)):
        last = (idx_ref[0] & 1) ^ n
        rows = pl.ds(pl.multiple_of(last * (4 * S - 8), 8), 8)
        copies.append(pltpu.make_async_copy(x_ref.at[rows, :], out.at[:, :CA], sem.at[2 * n]))
        rows = pl.ds(pl.multiple_of(last * (S - 8), 8), 8)
        copies.append(
            pltpu.make_async_copy(cot_ref.at[rows, :], out.at[:, CA:], sem.at[2 * n + 1])
        )
    for copy in copies:
        copy.start()
    for copy in copies:
        copy.wait()


def sides(idx_ref, chip_ref, core_ref, rows, lanes):
    chip = chip_ref[:, lanes].astype(F32)
    core = core_ref[:, lanes].astype(F32)
    even = (idx_ref[0] & 1) == 0
    before, behind = jnp.where(even, chip, core), jnp.where(even, core, chip)
    return before[8 - rows :], behind[:rows]


def act_kernel(
    x_ref, cot_ref, down_ref, temb_ref,
    xp_ref, act_ref, cot_out, down_out,
    xs_ref, xb_ref, sem,
):
    parts = []
    for k in range(4):
        rows = pl.ds(512 * k, 512)
        parts.append(pltpu.make_async_copy(x_ref.at[rows, :], xb_ref.at[rows, :], sem.at[k]))
    whole = [
        pltpu.make_async_copy(cot_ref, cot_out, sem.at[4]),
        pltpu.make_async_copy(down_ref, down_out, sem.at[5]),
    ]
    for copy in parts + whole:
        copy.start()
    for k in range(4):
        parts[k].wait()

        @pl.loop(0, 2)
        def _(n):
            i = 2 * k + n
            r = rows_of(i, 256)
            v = xb_ref[r, :].astype(F32)
            xs_ref[0, r, :] = v[:, :128]
            xs_ref[1, r, :] = v[:, 128:]
            r = rows_of(i, 64)
            for j in range(4):
                v = phase(xs_ref, i * 256 + j, 64)
                pre = v * rms(v) + temb_ref[...]
                lanes = slice(j * CA, (j + 1) * CA)
                xp_ref[r, lanes] = v.astype(BF16)
                act_ref[r, lanes] = (pre * sigmoid(pre)).astype(BF16)

    for copy in whole:
        copy.wait()


def forward_kernel(
    idx_ref, xp_ref, act_ref, chip_ref, core_ref, cot_ref, temb_ref, one_ref, down_ref,
    keep_ref, send_ref, mw_ref, uw_ref, ab_ref, co_ref,
    xs_ref, ubw_ref, at_ref,
):
    before, behind = sides(idx_ref, chip_ref, core_ref, 8, slice(0, CA))
    for h in range(2):
        lanes = slice(h * 128, (h + 1) * 128)
        xs_ref[h, :8, :] = behind[:, lanes]
        xs_ref[h, 8:56, :] = jnp.zeros((48, 128), F32)
        xs_ref[h, 56:, :] = before[:, lanes]
    inner = inside(idx_ref, S, E - S, 2)
    for j in range(4):
        v = phase(xs_ref, j, 16)
        pre = v * rms(v) + temb_ref[...]
        uw_ref[S:, (j + 1) * CA : (j + 2) * CA] = (pre * sigmoid(pre) * inner).astype(BF16)
    uw_ref[:S, CA : 5 * CA] = act_ref[...]
    uw_ref[:, :CA] = later(uw_ref[:, 4 * CA : 5 * CA].astype(F32)).astype(BF16)
    uw_ref[:, 5 * CA :] = sooner(uw_ref[:, CA : 2 * CA].astype(F32)).astype(BF16)
    for i in range(4):
        lanes = slice(i * 128, (i + 1) * 128)
        at_ref[lanes, :] = turned(cot_ref[:, lanes])

    for j in range(4):
        lanes = slice(j * CA, (j + 1) * CA)
        hidden = dot(uw_ref[:, j * CA : (j + 3) * CA], one_ref[...])
        mw_ref[:S, lanes] = (xp_ref[:, lanes].astype(F32) + hidden[:S]).astype(BF16)
        mw_ref[S:, lanes] = (phase(xs_ref, j, 16) + hidden[S:]).astype(BF16)
    for n in range(2):
        lanes = slice(n * CA, (n + 1) * CA)
        co_ref[:, lanes] = dot(mw_ref[...], down_ref[:, lanes]).astype(BF16)

    @pl.loop(0, 3)
    def _(i):
        r = rows_of(i, STEP)
        c32 = co_ref[r, :].astype(F32)
        normed = c32 * rms(c32)
        keep = inside(idx_ref, i * STEP, STEP, 1)
        ubw_ref[r, CB : 2 * CB] = (normed * sigmoid(normed) * keep).astype(BF16)

    act_b = ubw_ref[:, CB : 2 * CB]
    ab_ref[...] = act_b
    act_b = act_b.astype(F32)
    ubw_ref[:, :CB] = later(act_b).astype(BF16)
    ubw_ref[:, 2 * CB :] = sooner(act_b).astype(BF16)

    scaling = 1.0 / math.sqrt(16 * 32768)
    for n in range(6):
        two = dot(at_ref[...], ubw_ref[:S, n * CA : (n + 1) * CA]) * scaling
        for c in range(8):
            even, odd = two[64 * c : 64 * c + 32], two[64 * c + 32 : 64 * c + 64]
            put(idx_ref, keep_ref, send_ref, c % 4, c // 4, slice(None), even, odd, n * CA)


def coarse_kernel(
    idx_ref, co_ref, cot_ref, chip_ref, core_ref, down_ref, two_ref,
    dc_ref, dh_ref, dm_ref,
    cw_ref, back_ref,
):
    before, behind = sides(idx_ref, chip_ref, core_ref, 2, slice(CA, None))
    cot = jnp.concatenate(
        [cot_ref[...].astype(F32), behind, jnp.zeros((12, CB), F32), before], axis=0
    )
    cw_ref[:, CB : 2 * CB] = cot.astype(BF16)
    cw_ref[:, :CB] = sooner(cot).astype(BF16)
    cw_ref[:, 2 * CB :] = later(cot).astype(BF16)
    for n in range(2):
        lanes = slice(n * CA, (n + 1) * CA)
        back = dot_nt(cw_ref[:, :CB], two_ref[n * CA : (n + 1) * CA, :])
        back += dot_nt(cw_ref[:, CB : 2 * CB], two_ref[CB + n * CA : CB + (n + 1) * CA, :])
        back += dot_nt(cw_ref[:, 2 * CB :], two_ref[2 * CB + n * CA : 2 * CB + (n + 1) * CA, :])
        back_ref[:, lanes] = back

    @pl.loop(0, 3)
    def _(i):
        r = rows_of(i, STEP)
        c32 = co_ref[r, :].astype(F32)
        factor = rms(c32)
        normed = c32 * factor
        sig = sigmoid(normed)
        q = back_ref[r, :] * (sig * (1.0 + normed * (1.0 - sig)))
        m = jnp.mean(q * normed, -1, keepdims=True)
        grad = cw_ref[r, CB : 2 * CB].astype(F32) + factor * (q - normed * m)
        dc_ref[r, :] = (grad * inside(idx_ref, i * STEP, STEP, 1)).astype(BF16)

    for n in range(4):
        lanes = slice(n * CA, (n + 1) * CA)
        dm = dot_nt(dc_ref[...], down_ref[lanes, :])
        dm_ref[:, lanes] = dm[:S]
        dh_ref[:, lanes] = dm.astype(BF16)


def fine_kernel(
    idx_ref, xp_ref, dc_ref, dh_ref, mw_ref, uw_ref, temb_ref, emb_ref, one_ref,
    keep_ref, send_ref, dp_ref,
    dhw_ref, dt_ref, at_ref, dt_all_ref,
):
    scaling = 1.0 / math.sqrt(16 * 32768)
    dhw_ref[:, CA : 5 * CA] = dh_ref[...]
    dhw_ref[:, :CA] = later(dh_ref[:, 3 * CA :].astype(F32)).astype(BF16)
    dhw_ref[:, 5 * CA :] = sooner(dh_ref[:, :CA].astype(F32)).astype(BF16)
    dt_ref[...] = jnp.zeros((8, CA), F32)
    for i in range(4):
        lanes = slice(i * 128, (i + 1) * 128)
        at_ref[lanes, :] = turned(dc_ref[:S, lanes])
    for j in range(4):
        for i in range(2):
            lanes = slice(j * CA + i * 128, j * CA + (i + 1) * 128)
            dt_all_ref[i * 128 : (i + 1) * 128, j * S : (j + 1) * S] = turned(dh_ref[:S, lanes])

    @pl.loop(0, 2)
    def _(i):
        r = rows_of(i, 256)
        for j in range(4):
            lanes = slice(j * CA, (j + 1) * CA)
            back = dot_nt(dhw_ref[r, (j + 2) * CA : (j + 3) * CA], one_ref[:CA, :])
            back += dot_nt(dhw_ref[r, (j + 1) * CA : (j + 2) * CA], one_ref[CA : 2 * CA, :])
            back += dot_nt(dhw_ref[r, lanes], one_ref[2 * CA :, :])
            v = xp_ref[r, lanes].astype(F32)
            pre = v * rms(v) + temb_ref[...]
            sig = sigmoid(pre)
            d_pre = back * (sig * (1.0 + pre * (1.0 - sig)))
            dt_ref[...] += d_pre.reshape(32, 8, CA).sum(0)
            dp_ref[r, lanes] = d_pre

    for n in range(4):
        down = dot(at_ref[...], mw_ref[:S, n * CA : (n + 1) * CA]) * scaling
        for c in range(8):
            even, odd = down[64 * c : 64 * c + 32], down[64 * c + 32 : 64 * c + 64]
            put(idx_ref, keep_ref, send_ref, c % 4, c // 4, slice(0, 32), even, odd, n * CA)

    for n in range(4):
        if n < 3:
            one = jnp.zeros((CA, CA), F32)
            for j in range(4):
                lanes = slice((j + n) * CA, (j + n + 1) * CA)
                one += dot(dt_all_ref[:, j * S : (j + 1) * S], uw_ref[:S, lanes])
            one *= scaling
        else:
            dt = jnp.sum(dt_ref[...].T, axis=1, keepdims=True)
            one = dt * (emb_ref[...] * scaling)
        for c in range(8):
            even, odd = one[32 * c : 32 * c + 16], one[32 * c + 16 : 32 * c + 32]
            put(idx_ref, keep_ref, send_ref, c % 4, c // 4, slice(32, 48), even, odd, n * CA)


def signal_kernel(xp_ref, dm_ref, dp_ref, sg_ref, ys_ref):
    @pl.loop(0, 8)
    def _(i):
        r = rows_of(i, 64)
        for j in range(4):
            lanes = slice(j * CA, (j + 1) * CA)
            v = xp_ref[r, lanes].astype(F32)
            factor = rms(v)
            normed = v * factor
            d_pre = dp_ref[r, lanes]
            m = jnp.mean(d_pre * normed, -1, keepdims=True)
            grad = dm_ref[r, lanes] + factor * (d_pre - normed * m)
            ys_ref[0, pl.ds(i * 256 + j, 64, stride=4), :] = grad[:, :128]
            ys_ref[1, pl.ds(i * 256 + j, 64, stride=4), :] = grad[:, 128:]
        r = rows_of(i, 256)
        sg_ref[r, :128] = ys_ref[0, r, :].astype(BF16)
        sg_ref[r, 128:] = ys_ref[1, r, :].astype(BF16)


def encoded_kernel(co_ref, ab_ref, two_ref, enc_ref, ubw_ref):
    act_b = ab_ref[...].astype(F32)
    ubw_ref[:, CB : 2 * CB] = ab_ref[...]
    ubw_ref[:, :CB] = later(act_b).astype(BF16)
    ubw_ref[:, 2 * CB :] = sooner(act_b).astype(BF16)

    for n in range(2):
        lanes = slice(n * CA, (n + 1) * CA)
        enc = co_ref[:S, lanes].astype(F32) + dot(ubw_ref[:S, :], two_ref[:, lanes])
        enc_ref[:, lanes] = enc.astype(BF16)


def add_kernel(terms, *refs):
    at = 0
    for out in refs[terms:]:
        rows = slice(at, at + out.shape[0])
        total = refs[0][rows].astype(F32)
        for ref in refs[1:terms]:
            total = total + ref[rows].astype(F32)
        out[...] = total.astype(BF16)
        at += out.shape[0]


def join_kernel(own_u, got_u, own_v, got_v, own_ref, send_ref):
    half = own_u.shape[2]
    for own, got, lanes in (
        (own_u, got_u, slice(0, half)),
        (own_v, got_v, slice(half, 2 * half)),
    ):
        own_ref[:, lanes] = (own[0].astype(F32) + got[0].astype(F32)).astype(BF16)
        send_ref[:, lanes] = (own[1].astype(F32) + got[1].astype(F32)).astype(BF16)


def lines_kernel(a_ref, a_got, b_ref, b_got, out_ref):
    two = a_ref[0].astype(F32) + a_got[0].astype(F32)
    rest = b_ref[...].astype(F32) + b_got[...].astype(F32)
    for d in range(16):
        down = rest[:32, 64 * d : 64 * d + 64]
        last = rest[32:, 48 * d : 48 * d + 48]
        time = rest[32:, 3 * CA + 16 * d : 3 * CA + 16 * d + 16]
        top = jnp.concatenate([two[:, 96 * d : 96 * d + 96], down[:, :32]], axis=1)
        low = jnp.concatenate([down[:16, 32:], down[16:, 32:], last, time], axis=1)
        out_ref[d] = jnp.concatenate([top, low], axis=0).astype(BF16)


def last_kernel(in_ref, one_ref, down_ref, two_ref, time_ref):
    line = in_ref[0].astype(F32)
    for d in range(1, 16):
        line = line + in_ref[d].astype(F32)
    two_ref[...] = line[:32, :96]
    down_ref[:, :32] = line[:32, 96:]
    down_ref[:16, 32:] = line[32:, :32]
    down_ref[16:, 32:] = line[32:, 32:64]
    one_ref[...] = line[32:, 64:112]
    time_ref[...] = line[32:, 112:].T


def call(kernel, operands, outs, scratch=(), flops=0, nbytes=0, smem=False, far=0, sems=0,
         room=24):
    vmem = pl.BlockSpec(memory_space=pltpu.VMEM)
    return pl.pallas_call(
        kernel,
        in_specs=[pl.BlockSpec(memory_space=pltpu.SMEM)] * smem
        + [pl.BlockSpec(memory_space=pltpu.HBM)] * far
        + [vmem] * (len(operands) - far - smem),
        out_specs=[vmem] * len(outs),
        out_shape=[jax.ShapeDtypeStruct(shape, kind) for shape, kind in outs],
        scratch_shapes=[pltpu.VMEM(shape, kind) for shape, kind in scratch]
        + [pltpu.SemaphoreType.DMA((sems,))] * (sems > 0),
        cost_estimate=pl.CostEstimate(flops=flops, bytes_accessed=nbytes, transcendentals=0),
        compiler_params=pltpu.CompilerParams(vmem_limit_bytes=int(room * 2**20)),
    )(*operands)


def embed(stamps, width):
    half = width // 2
    freqs = jnp.exp(-math.log(10000.0) * jnp.arange(half, dtype=F32) / half)
    angles = stamps.astype(F32)[:, None] * freqs[None, :]
    return jnp.concatenate([jnp.sin(angles), jnp.cos(angles)], axis=-1)


def moved(value, target):
    pairs = [(i, target(i // 8, i // 2 % 4, i % 2)) for i in range(16)]
    return lax.ppermute(value, "tm", pairs)


def swap_core(v):
    return moved(v, lambda y, x, c: y * 8 + x * 2 + 1 - c)


def swap_x(v, apart):
    return moved(v, lambda y, x, c: y * 8 + (x ^ apart) * 2 + c)


def swap_y(v):
    pairs = [(i, i ^ (8 * 16 + 8)) for i in range(256)]
    return lax.ppermute(v, AXES, pairs)


def ring(parts):
    u, su, v, sv = parts
    gu = swap_x(su, 1)
    gv = swap_x(sv, 3)
    u, su = added([u, gu], (2, 2))
    v, sv = added([v, gv], (2, 2))
    gu = swap_x(su, 3)
    gv = swap_x(sv, 1)
    rows, half = u.shape[1:]
    own, send = call(
        join_kernel, [u, gu, v, gv], [((rows, 2 * half), BF16)] * 2,
        nbytes=600_000,
    )
    return own, swap_y(send)


def added(terms, cuts):
    tail = terms[0].shape[1:]
    size = math.prod(terms[0].shape) * 2
    return call(
        lambda *refs: add_kernel(len(terms), *refs), terms,
        [((n,) + tail, BF16) for n in cuts], nbytes=size * (len(terms) + 1),
    )


def per_device(signal, timesteps, cotangent, conv_one, down_proj, conv_two, time_proj):
    x, cot = signal[0], cotangent[0]
    tm = lax.axis_index("tm")
    idx = tm.astype(jnp.int32).reshape(1)
    for_chip, for_core = call(
        edges_kernel, [idx, x, cot], [((8, CA + CB), BF16)] * 2, nbytes=50_000,
        smem=True, far=2, sems=4, room=60,
    )
    chip = lax.ppermute(for_chip, "tm", [(i, i + 1 if i % 2 else i - 1) for i in range(1, 15)])
    core = lax.ppermute(for_core, "tm", [(i, i ^ 1) for i in range(16)])
    emb = embed(timesteps, EMB)
    temb = jnp.dot(emb, time_proj.astype(F32), precision=lax.Precision.HIGHEST)
    xp, act, cot, down_proj = call(
        act_kernel, [x, cot, down_proj, temb],
        [((S, 4 * CA), BF16)] * 2
        + [(v.shape, BF16) for v in (cot, down_proj)],
        [((2, 4 * S, 128), F32), ((4 * S, CA), BF16)], 50_000_000, 6_500_000, far=3, sems=6,
        room=48,
    )
    a_keep, a_send, mw, uw, ab, co = call(
        forward_kernel,
        [idx, xp, act, chip, core, cot, temb, conv_one, down_proj],
        [((8, 32, 3 * CB), BF16)] * 2
        + [((E, 4 * CA), BF16), ((E, 6 * CA), BF16), ((E, CB), BF16), ((E, CB), BF16)],
        [((2, 64, 128), F32), ((E, 3 * CB), BF16), ((CB, S), BF16)],
        2_200_000_000, 10_000_000, smem=True,
    )
    a_got = swap_core(a_send)
    dc, dh, dm = call(
        coarse_kernel, [idx, co, cot, chip, core, down_proj, conv_two],
        [((E, CB), BF16), ((E, 4 * CA), BF16), ((S, 4 * CA), F32)],
        [((E, 3 * CB), BF16), ((E, CB), F32)], 1_400_000_000, 7_000_000, smem=True,
    )
    a_own, a_send = added([a_keep, a_got], (4, 4))
    a_got = swap_x(a_send, 1)
    b_keep, b_send, d_pre = call(
        fine_kernel, [idx, xp, dc, dh, mw, uw, temb, emb, conv_one],
        [((16, 48, 2 * CA), BF16)] * 2 + [((S, 4 * CA), F32)],
        [((E, 6 * CA), BF16), ((8, CA), F32), ((CB, S), BF16), ((CA, 4 * S), BF16)],
        2_200_000_000, 11_000_000, smem=True,
    )
    b_got = swap_core(b_send)
    (encoded,) = call(
        encoded_kernel, [co, ab, conv_two], [((S, CB), BF16)],
        [((E, 3 * CB), BF16)], 800_000_000, 3_000_000,
    )
    (signal_grad,) = call(
        signal_kernel, [xp, dm, d_pre], [((4 * S, CA), BF16)],
        [((2, 4 * S, 128), F32)], 20_000_000, 6_000_000,
    )
    b_parts = added([b_keep, b_got], (4, 4, 4, 4))
    a_own, a_send = added([a_own, a_got], (2, 2))
    a_got = swap_x(a_send, 3)
    a_own, a_send = added([a_own, a_got], (1, 1))
    a_got = swap_y(a_send)
    b_own, b_got = ring(b_parts)
    (lines,) = call(
        lines_kernel, [a_own, a_got, b_own, b_got],
        [((16, 48, 128), BF16)], nbytes=900_000,
    )
    lines = lax.all_to_all(lines, "dp", 0, 0, tiled=True)
    outs = call(
        last_kernel, [lines],
        [((16, 48), F32), ((32, 64), F32), ((32, 96), F32), ((16, 16), F32)], nbytes=300_000,
    )
    one, down, two, time = outs
    return encoded[None], signal_grad[None], one.T, down.T, two.T, time


def solution(mesh):
    return jax.shard_map(
        per_device,
        mesh=mesh,
        in_specs=(P("dp", "tm", None), P("dp"), P("dp", "tm", None), P(), P(), P(), P()),
        out_specs=(
            P("dp", "tm", None),
            P("dp", "tm", None),
            P("dp", "tm"),
            P("dp", "tm"),
            P("dp", "tm"),
            P("dp", "tm"),
        ),
        check_vma=False,
    )
```

```python
import math

import jax
import jax.numpy as jnp
from jax import lax
from jax.experimental import pallas as pl
from jax.experimental.pallas import tpu as pltpu
from jax.sharding import PartitionSpec as P


EPS = 1e-06
CA, CB, EMB = 256, 512, 256
S = 512
E = 528
STEP = 176
F32, BF16 = jnp.float32, jnp.bfloat16
AXES = ("dp", "tm")
NT = (((1,), (1,)), ((), ()))


def dot(a, b):
    return jnp.dot(a, b, preferred_element_type=F32)


def dot_nt(a, b):
    return lax.dot_general(a, b, NT, preferred_element_type=F32)


def rows_of(i, size):
    return pl.ds(pl.multiple_of(i * size, 16), size)


def sigmoid(v):
    return 0.5 * jnp.tanh(0.5 * v) + 0.5


def inside(idx_ref, start, size, margin):
    row = lax.broadcasted_iota(jnp.int32, (size, 1), 0) + start
    past = jnp.logical_and(row >= S, row < S + margin)
    before = row >= E - margin
    off = jnp.logical_or(
        jnp.logical_and(past, idx_ref[0] == 15), jnp.logical_and(before, idx_ref[0] == 0)
    )
    return jnp.where(off, 0.0, 1.0)


def phase(ref, start, size):
    return jnp.concatenate([ref[h, pl.ds(start, size, stride=4), :] for h in range(2)], axis=1)


def later(v):
    return pltpu.roll(v, 1, 0)


def sooner(v):
    return pltpu.roll(v, v.shape[0] - 1, 0)


def places(idx_ref, xx, y):
    apart = xx ^ ((idx_ref[0] >> 1) & 3)
    side = y ^ (idx_ref[0] >> 3)
    first = jnp.where(apart == 3, 1, jnp.where(apart == 0, 0, apart + 1))
    second = jnp.where(apart < 2, apart, 5 - apart)
    return first * 2 + side, 8 + second * 2 + side


def put(idx_ref, keep_ref, send_ref, xx, y, rows, even, odd, at=0):
    core, half = idx_ref[0] & 1, keep_ref.shape[2]
    keep = jnp.where(core == 0, even, odd).astype(BF16)
    send = jnp.where(core == 0, odd, even).astype(BF16)
    for h, where in enumerate(places(idx_ref, xx, y)):
        low, high = max(at, h * half), min(at + even.shape[1], (h + 1) * half)
        if low < high:
            lanes = slice(low - h * half, high - h * half)
            keep_ref[where, rows, lanes] = keep[:, low - at : high - at]
            send_ref[where, rows, lanes] = send[:, low - at : high - at]


def rms(v):
    return lax.rsqrt(jnp.mean(v * v, -1, keepdims=True) + EPS)


def turned(v):
    return v.astype(F32).T.astype(BF16)


def edges_kernel(idx_ref, x_ref, cot_ref, one_ref, two_ref, sem):
    copies = []
    for n, out in enumerate((one_ref, two_ref)):
        last = (idx_ref[0] & 1) ^ n
        rows = pl.ds(pl.multiple_of(last * (4 * S - 8), 8), 8)
        copies.append(pltpu.make_async_copy(x_ref.at[rows, :], out.at[:, :CA], sem.at[2 * n]))
        rows = pl.ds(pl.multiple_of(last * (S - 8), 8), 8)
        copies.append(
            pltpu.make_async_copy(cot_ref.at[rows, :], out.at[:, CA:], sem.at[2 * n + 1])
        )
    for copy in copies:
        copy.start()
    for copy in copies:
        copy.wait()


def sides(idx_ref, chip_ref, core_ref, rows, lanes):
    chip = chip_ref[:, lanes].astype(F32)
    core = core_ref[:, lanes].astype(F32)
    even = (idx_ref[0] & 1) == 0
    before, behind = jnp.where(even, chip, core), jnp.where(even, core, chip)
    return before[8 - rows :], behind[:rows]


def act_kernel(
    x_ref, cot_ref, down_ref, temb_ref,
    xp_ref, act_ref, cot_out, down_out,
    xs_ref, xb_ref, sem,
):
    parts = []
    for k in range(4):
        rows = pl.ds(512 * k, 512)
        parts.append(pltpu.make_async_copy(x_ref.at[rows, :], xb_ref.at[rows, :], sem.at[k]))
    whole = [
        pltpu.make_async_copy(cot_ref, cot_out, sem.at[4]),
        pltpu.make_async_copy(down_ref, down_out, sem.at[5]),
    ]
    for copy in parts + whole:
        copy.start()
    for k in range(4):
        parts[k].wait()

        @pl.loop(0, 2)
        def _(n):
            i = 2 * k + n
            r = rows_of(i, 256)
            v = xb_ref[r, :].astype(F32)
            xs_ref[0, r, :] = v[:, :128]
            xs_ref[1, r, :] = v[:, 128:]
            r = rows_of(i, 64)
            for j in range(4):
                v = phase(xs_ref, i * 256 + j, 64)
                pre = v * rms(v) + temb_ref[...]
                lanes = slice(j * CA, (j + 1) * CA)
                xp_ref[r, lanes] = v.astype(BF16)
                act_ref[r, lanes] = (pre * sigmoid(pre)).astype(BF16)

    for copy in whole:
        copy.wait()


def forward_kernel(
    idx_ref, xp_ref, act_ref, chip_ref, core_ref, cot_ref, temb_ref, one_ref, down_ref,
    keep_ref, send_ref, mw_ref, uw_ref, ab_ref, co_ref,
    xs_ref, ubw_ref, at_ref,
):
    before, behind = sides(idx_ref, chip_ref, core_ref, 8, slice(0, CA))
    for h in range(2):
        lanes = slice(h * 128, (h + 1) * 128)
        xs_ref[h, :8, :] = behind[:, lanes]
        xs_ref[h, 8:56, :] = jnp.zeros((48, 128), F32)
        xs_ref[h, 56:, :] = before[:, lanes]
    inner = inside(idx_ref, S, E - S, 2)
    for j in range(4):
        v = phase(xs_ref, j, 16)
        pre = v * rms(v) + temb_ref[...]
        uw_ref[S:, (j + 1) * CA : (j + 2) * CA] = (pre * sigmoid(pre) * inner).astype(BF16)
    uw_ref[:S, CA : 5 * CA] = act_ref[...]
    uw_ref[:, :CA] = later(uw_ref[:, 4 * CA : 5 * CA].astype(F32)).astype(BF16)
    uw_ref[:, 5 * CA :] = sooner(uw_ref[:, CA : 2 * CA].astype(F32)).astype(BF16)
    for i in range(4):
        lanes = slice(i * 128, (i + 1) * 128)
        at_ref[lanes, :] = turned(cot_ref[:, lanes])

    for j in range(4):
        lanes = slice(j * CA, (j + 1) * CA)
        hidden = dot(uw_ref[:, j * CA : (j + 3) * CA], one_ref[...])
        mw_ref[:S, lanes] = (xp_ref[:, lanes].astype(F32) + hidden[:S]).astype(BF16)
        mw_ref[S:, lanes] = (phase(xs_ref, j, 16) + hidden[S:]).astype(BF16)
    for n in range(2):
        lanes = slice(n * CA, (n + 1) * CA)
        co_ref[:, lanes] = dot(mw_ref[...], down_ref[:, lanes]).astype(BF16)

    @pl.loop(0, 3)
    def _(i):
        r = rows_of(i, STEP)
        c32 = co_ref[r, :].astype(F32)
        normed = c32 * rms(c32)
        keep = inside(idx_ref, i * STEP, STEP, 1)
        ubw_ref[r, CB : 2 * CB] = (normed * sigmoid(normed) * keep).astype(BF16)

    act_b = ubw_ref[:, CB : 2 * CB]
    ab_ref[...] = act_b
    act_b = act_b.astype(F32)
    ubw_ref[:, :CB] = later(act_b).astype(BF16)
    ubw_ref[:, 2 * CB :] = sooner(act_b).astype(BF16)

    scaling = 1.0 / math.sqrt(16 * 32768)
    for n in range(6):
        two = dot(at_ref[...], ubw_ref[:S, n * CA : (n + 1) * CA]) * scaling
        for c in range(8):
            even, odd = two[64 * c : 64 * c + 32], two[64 * c + 32 : 64 * c + 64]
            put(idx_ref, keep_ref, send_ref, c % 4, c // 4, slice(None), even, odd, n * CA)


def coarse_kernel(
    idx_ref, co_ref, cot_ref, chip_ref, core_ref, down_ref, two_ref,
    dc_ref, dh_ref, dm_ref,
    cw_ref, back_ref,
):
    before, behind = sides(idx_ref, chip_ref, core_ref, 2, slice(CA, None))
    cot = jnp.concatenate(
        [cot_ref[...].astype(F32), behind, jnp.zeros((12, CB), F32), before], axis=0
    )
    cw_ref[:, CB : 2 * CB] = cot.astype(BF16)
    cw_ref[:, :CB] = sooner(cot).astype(BF16)
    cw_ref[:, 2 * CB :] = later(cot).astype(BF16)
    for n in range(2):
        lanes = slice(n * CA, (n + 1) * CA)
        back = dot_nt(cw_ref[:, :CB], two_ref[n * CA : (n + 1) * CA, :])
        back += dot_nt(cw_ref[:, CB : 2 * CB], two_ref[CB + n * CA : CB + (n + 1) * CA, :])
        back += dot_nt(cw_ref[:, 2 * CB :], two_ref[2 * CB + n * CA : 2 * CB + (n + 1) * CA, :])
        back_ref[:, lanes] = back

    @pl.loop(0, 3)
    def _(i):
        r = rows_of(i, STEP)
        c32 = co_ref[r, :].astype(F32)
        factor = rms(c32)
        normed = c32 * factor
        sig = sigmoid(normed)
        q = back_ref[r, :] * (sig * (1.0 + normed * (1.0 - sig)))
        m = jnp.mean(q * normed, -1, keepdims=True)
        grad = cw_ref[r, CB : 2 * CB].astype(F32) + factor * (q - normed * m)
        dc_ref[r, :] = (grad * inside(idx_ref, i * STEP, STEP, 1)).astype(BF16)

    for n in range(4):
        lanes = slice(n * CA, (n + 1) * CA)
        dm = dot_nt(dc_ref[...], down_ref[lanes, :])
        dm_ref[:, lanes] = dm[:S]
        dh_ref[:, lanes] = dm.astype(BF16)


def fine_kernel(
    idx_ref, xp_ref, dc_ref, dh_ref, mw_ref, uw_ref, temb_ref, emb_ref, one_ref,
    keep_ref, send_ref, dp_ref,
    dhw_ref, dt_ref, at_ref, dt_all_ref,
):
    scaling = 1.0 / math.sqrt(16 * 32768)
    dhw_ref[:, CA : 5 * CA] = dh_ref[...]
    dhw_ref[:, :CA] = later(dh_ref[:, 3 * CA :].astype(F32)).astype(BF16)
    dhw_ref[:, 5 * CA :] = sooner(dh_ref[:, :CA].astype(F32)).astype(BF16)
    dt_ref[...] = jnp.zeros((8, CA), F32)
    for i in range(4):
        lanes = slice(i * 128, (i + 1) * 128)
        at_ref[lanes, :] = turned(dc_ref[:S, lanes])
    for j in range(4):
        for i in range(2):
            lanes = slice(j * CA + i * 128, j * CA + (i + 1) * 128)
            dt_all_ref[i * 128 : (i + 1) * 128, j * S : (j + 1) * S] = turned(dh_ref[:S, lanes])

    @pl.loop(0, 2)
    def _(i):
        r = rows_of(i, 256)
        for j in range(4):
            lanes = slice(j * CA, (j + 1) * CA)
            back = dot_nt(dhw_ref[r, (j + 2) * CA : (j + 3) * CA], one_ref[:CA, :])
            back += dot_nt(dhw_ref[r, (j + 1) * CA : (j + 2) * CA], one_ref[CA : 2 * CA, :])
            back += dot_nt(dhw_ref[r, lanes], one_ref[2 * CA :, :])
            v = xp_ref[r, lanes].astype(F32)
            pre = v * rms(v) + temb_ref[...]
            sig = sigmoid(pre)
            d_pre = back * (sig * (1.0 + pre * (1.0 - sig)))
            dt_ref[...] += d_pre.reshape(32, 8, CA).sum(0)
            dp_ref[r, lanes] = d_pre

    for n in range(4):
        down = dot(at_ref[...], mw_ref[:S, n * CA : (n + 1) * CA]) * scaling
        for c in range(8):
            even, odd = down[64 * c : 64 * c + 32], down[64 * c + 32 : 64 * c + 64]
            put(idx_ref, keep_ref, send_ref, c % 4, c // 4, slice(0, 32), even, odd, n * CA)

    for n in range(4):
        if n < 3:
            one = jnp.zeros((CA, CA), F32)
            for j in range(4):
                lanes = slice((j + n) * CA, (j + n + 1) * CA)
                one += dot(dt_all_ref[:, j * S : (j + 1) * S], uw_ref[:S, lanes])
            one *= scaling
        else:
            dt = jnp.sum(dt_ref[...].T, axis=1, keepdims=True)
            one = dt * (emb_ref[...] * scaling)
        for c in range(8):
            even, odd = one[32 * c : 32 * c + 16], one[32 * c + 16 : 32 * c + 32]
            put(idx_ref, keep_ref, send_ref, c % 4, c // 4, slice(32, 48), even, odd, n * CA)


def signal_kernel(xp_ref, dm_ref, dp_ref, sg_ref, ys_ref):
    @pl.loop(0, 8)
    def _(i):
        r = rows_of(i, 64)
        for j in range(4):
            lanes = slice(j * CA, (j + 1) * CA)
            v = xp_ref[r, lanes].astype(F32)
            factor = rms(v)
            normed = v * factor
            d_pre = dp_ref[r, lanes]
            m = jnp.mean(d_pre * normed, -1, keepdims=True)
            grad = dm_ref[r, lanes] + factor * (d_pre - normed * m)
            ys_ref[0, pl.ds(i * 256 + j, 64, stride=4), :] = grad[:, :128]
            ys_ref[1, pl.ds(i * 256 + j, 64, stride=4), :] = grad[:, 128:]
        r = rows_of(i, 256)
        sg_ref[r, :128] = ys_ref[0, r, :].astype(BF16)
        sg_ref[r, 128:] = ys_ref[1, r, :].astype(BF16)


def encoded_kernel(co_ref, ab_ref, two_ref, enc_ref, ubw_ref):
    act_b = ab_ref[...].astype(F32)
    ubw_ref[:, CB : 2 * CB] = ab_ref[...]
    ubw_ref[:, :CB] = later(act_b).astype(BF16)
    ubw_ref[:, 2 * CB :] = sooner(act_b).astype(BF16)

    for n in range(2):
        lanes = slice(n * CA, (n + 1) * CA)
        enc = co_ref[:S, lanes].astype(F32) + dot(ubw_ref[:S, :], two_ref[:, lanes])
        enc_ref[:, lanes] = enc.astype(BF16)


def add_kernel(terms, *refs):
    at = 0
    for out in refs[terms:]:
        rows = slice(at, at + out.shape[0])
        total = refs[0][rows].astype(F32)
        for ref in refs[1:terms]:
            total = total + ref[rows].astype(F32)
        out[...] = total.astype(BF16)
        at += out.shape[0]


def join_kernel(own_u, got_u, own_v, got_v, own_ref, send_ref):
    half = own_u.shape[2]
    for own, got, lanes in (
        (own_u, got_u, slice(0, half)),
        (own_v, got_v, slice(half, 2 * half)),
    ):
        own_ref[:, lanes] = (own[0].astype(F32) + got[0].astype(F32)).astype(BF16)
        send_ref[:, lanes] = (own[1].astype(F32) + got[1].astype(F32)).astype(BF16)


def lines_kernel(a_ref, a_got, b_ref, b_got, out_ref):
    two = a_ref[...].astype(F32) + a_got[...].astype(F32)
    rest = b_ref[...].astype(F32) + b_got[...].astype(F32)
    for d in range(16):
        down = rest[:32, 64 * d : 64 * d + 64]
        last = rest[32:, 48 * d : 48 * d + 48]
        time = rest[32:, 3 * CA + 16 * d : 3 * CA + 16 * d + 16]
        top = jnp.concatenate([two[:, 96 * d : 96 * d + 96], down[:, :32]], axis=1)
        low = jnp.concatenate([down[:16, 32:], down[16:, 32:], last, time], axis=1)
        out_ref[d] = jnp.concatenate([top, low], axis=0).astype(BF16)


def last_kernel(in_ref, one_ref, down_ref, two_ref, time_ref):
    line = in_ref[0].astype(F32)
    for d in range(1, 16):
        line = line + in_ref[d].astype(F32)
    two_ref[...] = line[:32, :96]
    down_ref[:, :32] = line[:32, 96:]
    down_ref[:16, 32:] = line[32:, :32]
    down_ref[16:, 32:] = line[32:, 32:64]
    one_ref[...] = line[32:, 64:112]
    time_ref[...] = line[32:, 112:].T


def call(kernel, operands, outs, scratch=(), flops=0, nbytes=0, smem=False, far=0, sems=0,
         room=24):
    vmem = pl.BlockSpec(memory_space=pltpu.VMEM)
    return pl.pallas_call(
        kernel,
        in_specs=[pl.BlockSpec(memory_space=pltpu.SMEM)] * smem
        + [pl.BlockSpec(memory_space=pltpu.HBM)] * far
        + [vmem] * (len(operands) - far - smem),
        out_specs=[vmem] * len(outs),
        out_shape=[jax.ShapeDtypeStruct(shape, kind) for shape, kind in outs],
        scratch_shapes=[pltpu.VMEM(shape, kind) for shape, kind in scratch]
        + [pltpu.SemaphoreType.DMA((sems,))] * (sems > 0),
        cost_estimate=pl.CostEstimate(flops=flops, bytes_accessed=nbytes, transcendentals=0),
        compiler_params=pltpu.CompilerParams(vmem_limit_bytes=int(room * 2**20)),
    )(*operands)


def embed(stamps, width):
    half = width // 2
    freqs = jnp.exp(-math.log(10000.0) * jnp.arange(half, dtype=F32) / half)
    angles = stamps.astype(F32)[:, None] * freqs[None, :]
    return jnp.concatenate([jnp.sin(angles), jnp.cos(angles)], axis=-1)


def moved(value, target):
    pairs = [(i, target(i // 8, i // 2 % 4, i % 2)) for i in range(16)]
    return lax.ppermute(value, "tm", pairs)


def swap_core(v):
    return moved(v, lambda y, x, c: y * 8 + x * 2 + 1 - c)


def swap_x(v, apart):
    return moved(v, lambda y, x, c: y * 8 + (x ^ apart) * 2 + c)


def swap_y(v):
    pairs = [(i, i ^ (8 * 16 + 8)) for i in range(256)]
    return lax.ppermute(v, AXES, pairs)


def ring(parts):
    u, su, v, sv = parts
    gu = swap_x(su, 1)
    gv = swap_x(sv, 3)
    u, su = added([u, gu], (2, 2))
    v, sv = added([v, gv], (2, 2))
    gu = swap_x(su, 3)
    gv = swap_x(sv, 1)
    rows, half = u.shape[1:]
    own, send = call(
        join_kernel, [u, gu, v, gv], [((rows, 2 * half), BF16)] * 2,
        nbytes=600_000,
    )
    return own, swap_y(send)


def added(terms, cuts):
    tail = terms[0].shape[1:]
    size = math.prod(terms[0].shape) * 2
    return call(
        lambda *refs: add_kernel(len(terms), *refs), terms,
        [((n,) + tail, BF16) for n in cuts], nbytes=size * (len(terms) + 1),
    )


def per_device(signal, timesteps, cotangent, conv_one, down_proj, conv_two, time_proj):
    x, cot = signal[0], cotangent[0]
    tm = lax.axis_index("tm")
    idx = tm.astype(jnp.int32).reshape(1)
    for_chip, for_core = call(
        edges_kernel, [idx, x, cot], [((8, CA + CB), BF16)] * 2, nbytes=50_000,
        smem=True, far=2, sems=4, room=60,
    )
    chip = lax.ppermute(for_chip, "tm", [(i, i + 1 if i % 2 else i - 1) for i in range(1, 15)])
    core = lax.ppermute(for_core, "tm", [(i, i ^ 1) for i in range(16)])
    emb = embed(timesteps, EMB)
    temb = jnp.dot(emb, time_proj.astype(F32), precision=lax.Precision.HIGHEST)
    xp, act, cot, down_proj = call(
        act_kernel, [x, cot, down_proj, temb],
        [((S, 4 * CA), BF16)] * 2
        + [(v.shape, BF16) for v in (cot, down_proj)],
        [((2, 4 * S, 128), F32), ((4 * S, CA), BF16)], 50_000_000, 6_500_000, far=3, sems=6,
        room=48,
    )
    a_keep, a_send, mw, uw, ab, co = call(
        forward_kernel,
        [idx, xp, act, chip, core, cot, temb, conv_one, down_proj],
        [((16, 32, 3 * CB // 2), BF16)] * 2
        + [((E, 4 * CA), BF16), ((E, 6 * CA), BF16), ((E, CB), BF16), ((E, CB), BF16)],
        [((2, 64, 128), F32), ((E, 3 * CB), BF16), ((CB, S), BF16)],
        2_200_000_000, 10_000_000, smem=True,
    )
    a_got = swap_core(a_send)
    dc, dh, dm = call(
        coarse_kernel, [idx, co, cot, chip, core, down_proj, conv_two],
        [((E, CB), BF16), ((E, 4 * CA), BF16), ((S, 4 * CA), F32)],
        [((E, 3 * CB), BF16), ((E, CB), F32)], 1_400_000_000, 7_000_000, smem=True,
    )
    a_parts = added([a_keep, a_got], (4, 4, 4, 4))
    a_own, a_got = ring(a_parts)
    b_keep, b_send, d_pre = call(
        fine_kernel, [idx, xp, dc, dh, mw, uw, temb, emb, conv_one],
        [((16, 48, 2 * CA), BF16)] * 2 + [((S, 4 * CA), F32)],
        [((E, 6 * CA), BF16), ((8, CA), F32), ((CB, S), BF16), ((CA, 4 * S), BF16)],
        2_200_000_000, 11_000_000, smem=True,
    )
    b_got = swap_core(b_send)
    (encoded,) = call(
        encoded_kernel, [co, ab, conv_two], [((S, CB), BF16)],
        [((E, 3 * CB), BF16)], 800_000_000, 3_000_000,
    )
    (signal_grad,) = call(
        signal_kernel, [xp, dm, d_pre], [((4 * S, CA), BF16)],
        [((2, 4 * S, 128), F32)], 20_000_000, 6_000_000,
    )
    b_parts = added([b_keep, b_got], (4, 4, 4, 4))
    b_own, b_got = ring(b_parts)
    (lines,) = call(
        lines_kernel, [a_own, a_got, b_own, b_got],
        [((16, 48, 128), BF16)], nbytes=900_000,
    )
    lines = lax.all_to_all(lines, "dp", 0, 0, tiled=True)
    outs = call(
        last_kernel, [lines],
        [((16, 48), F32), ((32, 64), F32), ((32, 96), F32), ((16, 16), F32)], nbytes=300_000,
    )
    one, down, two, time = outs
    return encoded[None], signal_grad[None], one.T, down.T, two.T, time


def solution(mesh):
    return jax.shard_map(
        per_device,
        mesh=mesh,
        in_specs=(P("dp", "tm", None), P("dp"), P("dp", "tm", None), P(), P(), P(), P()),
        out_specs=(
            P("dp", "tm", None),
            P("dp", "tm", None),
            P("dp", "tm"),
            P("dp", "tm"),
            P("dp", "tm"),
            P("dp", "tm"),
        ),
        check_vma=False,
    )
```

```python
import math

import jax
import jax.numpy as jnp
from jax import lax
from jax.experimental import pallas as pl
from jax.experimental.pallas import tpu as pltpu
from jax.sharding import PartitionSpec as P


EPS = 1e-06
CA, CB, EMB = 256, 512, 256
S = 512
E = 528
STEP = 176
F32, BF16 = jnp.float32, jnp.bfloat16
AXES = ("dp", "tm")
NT = (((1,), (1,)), ((), ()))


def dot(a, b):
    return jnp.dot(a, b, preferred_element_type=F32)


def dot_nt(a, b):
    return lax.dot_general(a, b, NT, preferred_element_type=F32)


def rows_of(i, size):
    return pl.ds(pl.multiple_of(i * size, 16), size)


def sigmoid(v):
    return 0.5 * jnp.tanh(0.5 * v) + 0.5


def inside(idx_ref, start, size, margin):
    row = lax.broadcasted_iota(jnp.int32, (size, 1), 0) + start
    past = jnp.logical_and(row >= S, row < S + margin)
    before = row >= E - margin
    off = jnp.logical_or(
        jnp.logical_and(past, idx_ref[0] == 15), jnp.logical_and(before, idx_ref[0] == 0)
    )
    return jnp.where(off, 0.0, 1.0)


def phase(ref, start, size):
    return jnp.concatenate([ref[h, pl.ds(start, size, stride=4), :] for h in range(2)], axis=1)


def later(v):
    return pltpu.roll(v, 1, 0)


def sooner(v):
    return pltpu.roll(v, v.shape[0] - 1, 0)


def places(idx_ref, xx, y):
    apart = xx ^ ((idx_ref[0] >> 1) & 3)
    side = y ^ (idx_ref[0] >> 3)
    first = jnp.where(apart == 3, 1, jnp.where(apart == 0, 0, apart + 1))
    second = jnp.where(apart < 2, apart, 5 - apart)
    return first * 2 + side, 8 + second * 2 + side


def put(idx_ref, keep_ref, send_ref, xx, y, rows, even, odd, at=0):
    core, half = idx_ref[0] & 1, keep_ref.shape[2]
    keep = jnp.where(core == 0, even, odd).astype(BF16)
    send = jnp.where(core == 0, odd, even).astype(BF16)
    for h, where in enumerate(places(idx_ref, xx, y)):
        low, high = max(at, h * half), min(at + even.shape[1], (h + 1) * half)
        if low < high:
            lanes = slice(low - h * half, high - h * half)
            keep_ref[where, rows, lanes] = keep[:, low - at : high - at]
            send_ref[where, rows, lanes] = send[:, low - at : high - at]


def rms(v):
    return lax.rsqrt(jnp.mean(v * v, -1, keepdims=True) + EPS)


def turned(v):
    return v.astype(F32).T.astype(BF16)


def edges_kernel(idx_ref, x_ref, cot_ref, one_ref, two_ref, sem):
    copies = []
    for n, out in enumerate((one_ref, two_ref)):
        last = (idx_ref[0] & 1) ^ n
        rows = pl.ds(pl.multiple_of(last * (4 * S - 8), 8), 8)
        copies.append(pltpu.make_async_copy(x_ref.at[rows, :], out.at[:, :CA], sem.at[2 * n]))
        rows = pl.ds(pl.multiple_of(last * (S - 8), 8), 8)
        copies.append(
            pltpu.make_async_copy(cot_ref.at[rows, :], out.at[:, CA:], sem.at[2 * n + 1])
        )
    for copy in copies:
        copy.start()
    for copy in copies:
        copy.wait()


def sides(idx_ref, chip_ref, core_ref, rows, lanes):
    chip = chip_ref[:, lanes].astype(F32)
    core = core_ref[:, lanes].astype(F32)
    even = (idx_ref[0] & 1) == 0
    before, behind = jnp.where(even, chip, core), jnp.where(even, core, chip)
    return before[8 - rows :], behind[:rows]


def act_kernel(
    x_ref, cot_ref, down_ref, temb_ref,
    xp_ref, act_ref, cot_out, down_out,
    xs_ref, xb_ref, sem,
):
    parts = []
    for k in range(4):
        rows = pl.ds(512 * k, 512)
        parts.append(pltpu.make_async_copy(x_ref.at[rows, :], xb_ref.at[rows, :], sem.at[k]))
    whole = [
        pltpu.make_async_copy(cot_ref, cot_out, sem.at[4]),
        pltpu.make_async_copy(down_ref, down_out, sem.at[5]),
    ]
    for copy in parts + whole:
        copy.start()
    for k in range(4):
        parts[k].wait()

        @pl.loop(0, 2)
        def _(n):
            i = 2 * k + n
            r = rows_of(i, 256)
            v = xb_ref[r, :].astype(F32)
            xs_ref[0, r, :] = v[:, :128]
            xs_ref[1, r, :] = v[:, 128:]
            r = rows_of(i, 64)
            for j in range(4):
                v = phase(xs_ref, i * 256 + j, 64)
                pre = v * rms(v) + temb_ref[...]
                lanes = slice(j * CA, (j + 1) * CA)
                xp_ref[r, lanes] = v.astype(BF16)
                act_ref[r, lanes] = (pre * sigmoid(pre)).astype(BF16)

    for copy in whole:
        copy.wait()


def forward_kernel(
    idx_ref, xp_ref, act_ref, chip_ref, core_ref, cot_ref, temb_ref, one_ref, down_ref,
    keep_ref, send_ref, mw_ref, uw_ref, ab_ref, co_ref,
    xs_ref, ubw_ref, at_ref,
):
    before, behind = sides(idx_ref, chip_ref, core_ref, 8, slice(0, CA))
    for h in range(2):
        lanes = slice(h * 128, (h + 1) * 128)
        xs_ref[h, :8, :] = behind[:, lanes]
        xs_ref[h, 8:56, :] = jnp.zeros((48, 128), F32)
        xs_ref[h, 56:, :] = before[:, lanes]
    inner = inside(idx_ref, S, E - S, 2)
    for j in range(4):
        v = phase(xs_ref, j, 16)
        pre = v * rms(v) + temb_ref[...]
        uw_ref[S:, (j + 1) * CA : (j + 2) * CA] = (pre * sigmoid(pre) * inner).astype(BF16)
    uw_ref[:S, CA : 5 * CA] = act_ref[...]
    uw_ref[:, :CA] = later(uw_ref[:, 4 * CA : 5 * CA].astype(F32)).astype(BF16)
    uw_ref[:, 5 * CA :] = sooner(uw_ref[:, CA : 2 * CA].astype(F32)).astype(BF16)
    for i in range(4):
        lanes = slice(i * 128, (i + 1) * 128)
        at_ref[lanes, :] = turned(cot_ref[:, lanes])

    for j in range(4):
        lanes = slice(j * CA, (j + 1) * CA)
        hidden = dot(uw_ref[:, j * CA : (j + 3) * CA], one_ref[...])
        mw_ref[:S, lanes] = (xp_ref[:, lanes].astype(F32) + hidden[:S]).astype(BF16)
        mw_ref[S:, lanes] = (phase(xs_ref, j, 16) + hidden[S:]).astype(BF16)
    for n in range(2):
        lanes = slice(n * CA, (n + 1) * CA)
        co_ref[:, lanes] = dot(mw_ref[...], down_ref[:, lanes]).astype(BF16)

    @pl.loop(0, 3)
    def _(i):
        r = rows_of(i, STEP)
        c32 = co_ref[r, :].astype(F32)
        normed = c32 * rms(c32)
        keep = inside(idx_ref, i * STEP, STEP, 1)
        ubw_ref[r, CB : 2 * CB] = (normed * sigmoid(normed) * keep).astype(BF16)

    act_b = ubw_ref[:, CB : 2 * CB]
    ab_ref[...] = act_b
    act_b = act_b.astype(F32)
    ubw_ref[:, :CB] = later(act_b).astype(BF16)
    ubw_ref[:, 2 * CB :] = sooner(act_b).astype(BF16)

    scaling = 1.0 / math.sqrt(16 * 32768)
    for n in range(6):
        two = dot(at_ref[...], ubw_ref[:S, n * CA : (n + 1) * CA]) * scaling
        for c in range(8):
            even, odd = two[64 * c : 64 * c + 32], two[64 * c + 32 : 64 * c + 64]
            put(idx_ref, keep_ref, send_ref, c % 4, c // 4, slice(None), even, odd, n * CA)


def coarse_kernel(
    idx_ref, co_ref, cot_ref, chip_ref, core_ref, down_ref, two_ref,
    dc_ref, dh_ref, dm_ref,
    cw_ref, back_ref,
):
    before, behind = sides(idx_ref, chip_ref, core_ref, 2, slice(CA, None))
    cot = jnp.concatenate(
        [cot_ref[...].astype(F32), behind, jnp.zeros((12, CB), F32), before], axis=0
    )
    cw_ref[:, CB : 2 * CB] = cot.astype(BF16)
    cw_ref[:, :CB] = sooner(cot).astype(BF16)
    cw_ref[:, 2 * CB :] = later(cot).astype(BF16)
    for n in range(2):
        lanes = slice(n * CA, (n + 1) * CA)
        back = dot_nt(cw_ref[:, :CB], two_ref[n * CA : (n + 1) * CA, :])
        back += dot_nt(cw_ref[:, CB : 2 * CB], two_ref[CB + n * CA : CB + (n + 1) * CA, :])
        back += dot_nt(cw_ref[:, 2 * CB :], two_ref[2 * CB + n * CA : 2 * CB + (n + 1) * CA, :])
        back_ref[:, lanes] = back

    @pl.loop(0, 3)
    def _(i):
        r = rows_of(i, STEP)
        c32 = co_ref[r, :].astype(F32)
        factor = rms(c32)
        normed = c32 * factor
        sig = sigmoid(normed)
        q = back_ref[r, :] * (sig * (1.0 + normed * (1.0 - sig)))
        m = jnp.mean(q * normed, -1, keepdims=True)
        grad = cw_ref[r, CB : 2 * CB].astype(F32) + factor * (q - normed * m)
        dc_ref[r, :] = (grad * inside(idx_ref, i * STEP, STEP, 1)).astype(BF16)

    for n in range(4):
        lanes = slice(n * CA, (n + 1) * CA)
        dm = dot_nt(dc_ref[...], down_ref[lanes, :])
        dm_ref[:, lanes] = dm[:S]
        dh_ref[:, lanes] = dm.astype(BF16)


def fine_kernel(
    idx_ref, xp_ref, dc_ref, dh_ref, mw_ref, uw_ref, temb_ref, emb_ref, one_ref,
    keep_ref, send_ref, dp_ref,
    dhw_ref, dt_ref, at_ref, dt_all_ref,
):
    scaling = 1.0 / math.sqrt(16 * 32768)
    dhw_ref[:, CA : 5 * CA] = dh_ref[...]
    dhw_ref[:, :CA] = later(dh_ref[:, 3 * CA :].astype(F32)).astype(BF16)
    dhw_ref[:, 5 * CA :] = sooner(dh_ref[:, :CA].astype(F32)).astype(BF16)
    dt_ref[...] = jnp.zeros((8, CA), F32)
    for i in range(4):
        lanes = slice(i * 128, (i + 1) * 128)
        at_ref[lanes, :] = turned(dc_ref[:S, lanes])
    for j in range(4):
        for i in range(2):
            lanes = slice(j * CA + i * 128, j * CA + (i + 1) * 128)
            dt_all_ref[i * 128 : (i + 1) * 128, j * S : (j + 1) * S] = turned(dh_ref[:S, lanes])

    @pl.loop(0, 2)
    def _(i):
        r = rows_of(i, 256)
        for j in range(4):
            lanes = slice(j * CA, (j + 1) * CA)
            back = dot_nt(dhw_ref[r, (j + 2) * CA : (j + 3) * CA], one_ref[:CA, :])
            back += dot_nt(dhw_ref[r, (j + 1) * CA : (j + 2) * CA], one_ref[CA : 2 * CA, :])
            back += dot_nt(dhw_ref[r, lanes], one_ref[2 * CA :, :])
            v = xp_ref[r, lanes].astype(F32)
            pre = v * rms(v) + temb_ref[...]
            sig = sigmoid(pre)
            d_pre = back * (sig * (1.0 + pre * (1.0 - sig)))
            dt_ref[...] += d_pre.reshape(32, 8, CA).sum(0)
            dp_ref[r, lanes] = d_pre

    for n in range(4):
        down = dot(at_ref[...], mw_ref[:S, n * CA : (n + 1) * CA]) * scaling
        for c in range(8):
            even, odd = down[64 * c : 64 * c + 32], down[64 * c + 32 : 64 * c + 64]
            put(idx_ref, keep_ref, send_ref, c % 4, c // 4, slice(0, 32), even, odd, n * CA)

    def place(value, at):
        for c in range(8):
            even, odd = value[32 * c : 32 * c + 16], value[32 * c + 16 : 32 * c + 32]
            put(idx_ref, keep_ref, send_ref, c % 4, c // 4, slice(32, 48), even, odd, at)

    for n in range(3):
        one = jnp.zeros((CA, CA), F32)
        for j in range(4):
            lanes = slice((j + n) * CA, (j + n + 1) * CA)
            one += dot(dt_all_ref[:, j * S : (j + 1) * S], uw_ref[:S, lanes])
        one *= scaling
        if n == 1:
            place(one[:, :128], 256)
            place(one[:, 128:], 512)
        else:
            place(one, 320 * n)
    time = jnp.sum(dt_ref[...].T, axis=1, keepdims=True) * (emb_ref[...] * scaling)
    place(time[:, :128], 384)
    place(time[:, 128:], 896)


def signal_kernel(xp_ref, dm_ref, dp_ref, sg_ref, ys_ref):
    @pl.loop(0, 8)
    def _(i):
        r = rows_of(i, 64)
        for j in range(4):
            lanes = slice(j * CA, (j + 1) * CA)
            v = xp_ref[r, lanes].astype(F32)
            factor = rms(v)
            normed = v * factor
            d_pre = dp_ref[r, lanes]
            m = jnp.mean(d_pre * normed, -1, keepdims=True)
            grad = dm_ref[r, lanes] + factor * (d_pre - normed * m)
            ys_ref[0, pl.ds(i * 256 + j, 64, stride=4), :] = grad[:, :128]
            ys_ref[1, pl.ds(i * 256 + j, 64, stride=4), :] = grad[:, 128:]
        r = rows_of(i, 256)
        sg_ref[r, :128] = ys_ref[0, r, :].astype(BF16)
        sg_ref[r, 128:] = ys_ref[1, r, :].astype(BF16)


def encoded_kernel(co_ref, ab_ref, two_ref, enc_ref, ubw_ref):
    act_b = ab_ref[...].astype(F32)
    ubw_ref[:, CB : 2 * CB] = ab_ref[...]
    ubw_ref[:, :CB] = later(act_b).astype(BF16)
    ubw_ref[:, 2 * CB :] = sooner(act_b).astype(BF16)

    for n in range(2):
        lanes = slice(n * CA, (n + 1) * CA)
        enc = co_ref[:S, lanes].astype(F32) + dot(ubw_ref[:S, :], two_ref[:, lanes])
        enc_ref[:, lanes] = enc.astype(BF16)


def add_kernel(terms, *refs):
    at = 0
    for out in refs[terms:]:
        rows = slice(at, at + out.shape[0])
        total = refs[0][rows].astype(F32)
        for ref in refs[1:terms]:
            total = total + ref[rows].astype(F32)
        out[...] = total.astype(BF16)
        at += out.shape[0]


def join_kernel(dp_ref, *refs):
    parts, outs = refs[:8], refs[8:]

    def packed(side, half):
        a, b = (
            parts[k][side].astype(F32) + parts[k + 1][side].astype(F32)
            for k in (2 * half, 4 + 2 * half)
        )
        top = jnp.concatenate([a, b[:32, :CA]], axis=1)
        low = jnp.concatenate([b[:16, CA:], b[16:32, CA:], b[32:]], axis=1)
        return jnp.concatenate([top, low], axis=0)

    first = dp_ref[0] < 8
    for side in range(2):
        zero, one = packed(side, 0), packed(side, 1)
        outs[2 * side][...] = jnp.where(first, zero, one).astype(BF16)
        outs[2 * side + 1][...] = jnp.where(first, one, zero).astype(BF16)


def lines_kernel(own_ref, lo_ref, hi_ref, both_ref, out_ref):
    total = own_ref[...].astype(F32) + lo_ref[...].astype(F32)
    total = total + hi_ref[...].astype(F32) + both_ref[...].astype(F32)
    two, last = total[:32, : 3 * CA], total[32:, 2 * CA :]
    rest = jnp.concatenate([total[32:, :CA], total[32:, CA : 2 * CA]], axis=0)
    rest = jnp.concatenate([total[:32, 3 * CA :], rest], axis=1)
    for d in range(8):
        down = rest[:, 64 * d : 64 * d + 64]
        one = last[:, 48 * d : 48 * d + 48]
        time = last[:, 384 + 16 * d : 384 + 16 * d + 16]
        top = jnp.concatenate([two[:, 96 * d : 96 * d + 96], down[:, :32]], axis=1)
        low = jnp.concatenate([down[:16, 32:], down[16:, 32:], one, time], axis=1)
        out_ref[d] = jnp.concatenate([top, low], axis=0).astype(BF16)


def last_kernel(in_ref, one_ref, down_ref, two_ref, time_ref):
    line = in_ref[0].astype(F32)
    for d in range(1, 8):
        line = line + in_ref[d].astype(F32)
    two_ref[...] = line[:32, :96]
    down_ref[:, :32] = line[:32, 96:]
    down_ref[:16, 32:] = line[32:, :32]
    down_ref[16:, 32:] = line[32:, 32:64]
    one_ref[...] = line[32:, 64:112]
    time_ref[...] = line[32:, 112:].T


def call(kernel, operands, outs, scratch=(), flops=0, nbytes=0, smem=False, far=0, sems=0,
         room=24):
    vmem = pl.BlockSpec(memory_space=pltpu.VMEM)
    return pl.pallas_call(
        kernel,
        in_specs=[pl.BlockSpec(memory_space=pltpu.SMEM)] * smem
        + [pl.BlockSpec(memory_space=pltpu.HBM)] * far
        + [vmem] * (len(operands) - far - smem),
        out_specs=[vmem] * len(outs),
        out_shape=[jax.ShapeDtypeStruct(shape, kind) for shape, kind in outs],
        scratch_shapes=[pltpu.VMEM(shape, kind) for shape, kind in scratch]
        + [pltpu.SemaphoreType.DMA((sems,))] * (sems > 0),
        cost_estimate=pl.CostEstimate(flops=flops, bytes_accessed=nbytes, transcendentals=0),
        compiler_params=pltpu.CompilerParams(vmem_limit_bytes=int(room * 2**20)),
    )(*operands)


def embed(stamps, width):
    half = width // 2
    freqs = jnp.exp(-math.log(10000.0) * jnp.arange(half, dtype=F32) / half)
    angles = stamps.astype(F32)[:, None] * freqs[None, :]
    return jnp.concatenate([jnp.sin(angles), jnp.cos(angles)], axis=-1)


def moved(value, target):
    pairs = [(i, target(i // 8, i // 2 % 4, i % 2)) for i in range(16)]
    return lax.ppermute(value, "tm", pairs)


def swap_core(v):
    return moved(v, lambda y, x, c: y * 8 + x * 2 + 1 - c)


def swap_x(v, apart):
    return moved(v, lambda y, x, c: y * 8 + (x ^ apart) * 2 + c)


def swap_y(v, apart):
    flip = 128 * (apart & 1) + 8 * (apart >> 1)
    return lax.ppermute(v, AXES, [(i, i ^ flip) for i in range(256)])


def ring(parts):
    u, su, v, sv = parts
    gu = swap_x(su, 1)
    gv = swap_x(sv, 3)
    u, su = added([u, gu], (2, 2))
    v, sv = added([v, gv], (2, 2))
    gu = swap_x(su, 3)
    gv = swap_x(sv, 1)
    return [u, gu, v, gv]


def added(terms, cuts):
    tail = terms[0].shape[1:]
    size = math.prod(terms[0].shape) * 2
    return call(
        lambda *refs: add_kernel(len(terms), *refs), terms,
        [((n,) + tail, BF16) for n in cuts], nbytes=size * (len(terms) + 1), room=12,
    )


def per_device(signal, timesteps, cotangent, conv_one, down_proj, conv_two, time_proj):
    x, cot = signal[0], cotangent[0]
    tm = lax.axis_index("tm")
    idx = tm.astype(jnp.int32).reshape(1)
    for_chip, for_core = call(
        edges_kernel, [idx, x, cot], [((8, CA + CB), BF16)] * 2, nbytes=50_000,
        smem=True, far=2, sems=4, room=60,
    )
    chip = lax.ppermute(for_chip, "tm", [(i, i + 1 if i % 2 else i - 1) for i in range(1, 15)])
    core = lax.ppermute(for_core, "tm", [(i, i ^ 1) for i in range(16)])
    emb = embed(timesteps, EMB)
    temb = jnp.dot(emb, time_proj.astype(F32), precision=lax.Precision.HIGHEST)
    xp, act, cot, down_proj = call(
        act_kernel, [x, cot, down_proj, temb],
        [((S, 4 * CA), BF16)] * 2
        + [(v.shape, BF16) for v in (cot, down_proj)],
        [((2, 4 * S, 128), F32), ((4 * S, CA), BF16)], 50_000_000, 6_500_000, far=3, sems=6,
        room=48,
    )
    a_keep, a_send, mw, uw, ab, co = call(
        forward_kernel,
        [idx, xp, act, chip, core, cot, temb, conv_one, down_proj],
        [((16, 32, 3 * CB // 2), BF16)] * 2
        + [((E, 4 * CA), BF16), ((E, 6 * CA), BF16), ((E, CB), BF16), ((E, CB), BF16)],
        [((2, 64, 128), F32), ((E, 3 * CB), BF16), ((CB, S), BF16)],
        2_200_000_000, 10_000_000, smem=True,
    )
    a_got = swap_core(a_send)
    dc, dh, dm = call(
        coarse_kernel, [idx, co, cot, chip, core, down_proj, conv_two],
        [((E, CB), BF16), ((E, 4 * CA), BF16), ((S, 4 * CA), F32)],
        [((E, 3 * CB), BF16), ((E, CB), F32)], 1_400_000_000, 7_000_000, smem=True,
    )
    a_parts = added([a_keep, a_got], (4, 4, 4, 4))
    a_parts = ring(a_parts)
    b_keep, b_send, d_pre = call(
        fine_kernel, [idx, xp, dc, dh, mw, uw, temb, emb, conv_one],
        [((16, 48, 2 * CA), BF16)] * 2 + [((S, 4 * CA), F32)],
        [((E, 6 * CA), BF16), ((8, CA), F32), ((CB, S), BF16), ((CA, 4 * S), BF16)],
        2_200_000_000, 11_000_000, smem=True,
    )
    b_got = swap_core(b_send)
    (encoded,) = call(
        encoded_kernel, [co, ab, conv_two], [((S, CB), BF16)],
        [((E, 3 * CB), BF16)], 800_000_000, 3_000_000,
    )
    (signal_grad,) = call(
        signal_kernel, [xp, dm, d_pre], [((4 * S, CA), BF16)],
        [((2, 4 * S, 128), F32)], 20_000_000, 6_000_000,
    )
    b_parts = added([b_keep, b_got], (4, 4, 4, 4))
    b_parts = ring(b_parts)
    dp = lax.axis_index("dp").astype(jnp.int32).reshape(1)
    parts = call(
        join_kernel, [dp, *a_parts, *b_parts], [((48, 4 * CA), BF16)] * 4,
        nbytes=1_200_000, smem=True, room=12,
    )
    got = [swap_y(parts[k], k) for k in (1, 2, 3)]
    (lines,) = call(lines_kernel, [parts[0], *got], [((8, 48, 128), BF16)], nbytes=500_000, room=12)
    groups = [list(range(8)), list(range(8, 16))]
    lines = lax.all_to_all(lines, "dp", 0, 0, tiled=True, axis_index_groups=groups)
    outs = call(
        last_kernel, [lines],
        [((16, 48), F32), ((32, 64), F32), ((32, 96), F32), ((16, 16), F32)], nbytes=300_000,
    )
    one, down, two, time = outs
    return encoded[None], signal_grad[None], one.T, down.T, two.T, time


def solution(mesh):
    return jax.shard_map(
        per_device,
        mesh=mesh,
        in_specs=(P("dp", "tm", None), P("dp"), P("dp", "tm", None), P(), P(), P(), P()),
        out_specs=(
            P("dp", "tm", None),
            P("dp", "tm", None),
            P("dp", "tm"),
            P("dp", "tm"),
            P("dp", "tm"),
            P("dp", "tm"),
        ),
        check_vma=False,
    )
```
